256 devices in a mesh: ctx: 16 (over x, y_hi, core), grp: 16 (over y_lo, z).
Axes of the slice: x: 4, y: 4 (y_hi: 2, y_lo: 2; y = y_hi * 2 + y_lo), z: 8, core: 2. Of those that a mesh axis runs over, the one named last changes fastest.
Arguments:
- tokens: bfloat16 [65536, 2560], P(('ctx', 'grp')), may hold values from -6 to 6
- norm_gain: bfloat16 [2560], replicated, may hold values from 0.5 to 1.5
- w_query: bfloat16 [2560, 2560], P('grp'), may hold values from -0.125 to 0.125
- w_key: bfloat16 [2560, 512], P('grp'), may hold values from -0.125 to 0.125
- w_value: bfloat16 [2560, 512], P('grp'), may hold values from -0.125 to 0.125
- b_query: bfloat16 [2560], replicated, may hold values from -3 to 3
- b_key: bfloat16 [512], replicated, may hold values from -3 to 3
- b_value: bfloat16 [512], replicated, may hold values from -3 to 3
- cache_keys: bfloat16 [2048, 512], P('ctx'), may hold values from -140 to 140
- cache_values: bfloat16 [2048, 512], P('ctx'), may hold values from -6 to 6
- block_lists: int32 [20, 512, 4], P(None, ('ctx', 'grp')), may hold values from -1 to 15, as said below
- start_position: int32 [1], replicated, may hold values from 0 to 983040
Outputs:
- context: float32 [65536, 2560], P(('ctx', 'grp'))
- keys_new: float32 [65536, 512], P(('ctx', 'grp'))
- values_new: float32 [65536, 512], P(('ctx', 'grp'))
The draws below stay inside these ranges and needn't reach their ends.
Inputs may be any that keep to these rules, and one draw needn't show every extreme that they name: `block_lists`: each list names distinct blocks of 128 prefix positions, named blocks first and -1 in the empty slots after them; every list names at least one block, some list names 4 and some only one.
All inputs are finite; a program needn't handle non-finite values.
Results may differ from the reference program's by a relative error of at most 0.034.
Values may be sent and summed in bfloat16 or wider, within the bound.
A program may use at most 128 MiB of HBM per device.

```python
import jax
import jax.numpy as jnp
import numpy as np
from jax import lax

D = 2560
HD = 128
KVH = 4
GROUP = 5
QBLK = 128
SEL = 4
ASKER_CHANNELS = 20
TOKENS = 65536
PREFIX = 2048
NQB = 512
LEADING_TILES = 16


def draw_block_lists(key, part):
    key_noise, key_vertical, lookup_self_share, key_count = jax.random.split(key, 4)
    noisy_affinity_share = jax.random.randint(key_noise, (ASKER_CHANNELS, NQB, LEADING_TILES), 0, 1000)
    vertical_band = (jax.random.randint(key_vertical, (ASKER_CHANNELS, 1, LEADING_TILES), 0, 5) == 0).astype(jnp.int32) * 1500
    latest_element = (jnp.arange(LEADING_TILES) == LEADING_TILES - 1).astype(jnp.int32)
    self_match_reward = jax.random.randint(lookup_self_share, (ASKER_CHANNELS, 1, 1), 0, 2) * 3000
    self_match_reward = self_match_reward.at[0].set(3000)
    attention_affinity = (noisy_affinity_share + vertical_band + self_match_reward * latest_element[None, None, :]) * LEADING_TILES + jnp.arange(LEADING_TILES, dtype=jnp.int32)[None, None, :]
    chosen = lax.top_k(attention_affinity, SEL)[1].astype(jnp.int32)
    counts = jax.random.randint(key_count, (ASKER_CHANNELS, NQB, 1), 1, SEL + 1)
    counts = counts.at[0, 0, 0].set(SEL).at[0, NQB - 1, 0].set(1)
    slot_index = jnp.arange(SEL, dtype=jnp.int32)[None, None, :]
    return jnp.where(slot_index < counts, chosen, -1).astype(jnp.int32)


def draw_cache_keys(key, part):
    key_base = jax.random.fold_in(key, 0)
    width_all = KVH * HD
    return jax.random.truncated_normal(key_base, -4.0, 4.0, (PREFIX, width_all), jnp.float32).astype(jnp.bfloat16)


def block_scale(stream_key, shape, cuts, low, largest):
    factor_of = 1.0
    for axis_at, blocks in cuts:
        heights = jax.random.uniform(jax.random.fold_in(jax.random.fold_in(stream_key, 6), axis_at), (blocks,), jnp.float32, low / len(cuts), largest / len(cuts))
        factor_of = factor_of * jnp.repeat(jnp.exp(heights), shape[axis_at] // blocks).reshape((-1,) + (1,) * (len(shape) - 1 - axis_at))
    return factor_of


def centred(stream_key, dims, scale, bound, cuts=(), held_as=jnp.bfloat16):
    values = jax.random.normal(stream_key, dims, jnp.float32) * scale
    if len(cuts) > 0:
        values = block_scale(stream_key, dims, cuts, -0.22, 0.18) * values
    return jnp.clip(values, min=-bound, max=bound).astype(held_as)


def setup_inputs(seed: int = 0) -> dict:
    streams_of = jax.random.split(jax.random.key(seed), 13)
    return {
        "tokens": centred(streams_of[0], (TOKENS, D), 1.0, 6.0, ((0, 256),)),
        "norm_gain": jnp.clip(1.0 + 0.1 * jax.random.normal(streams_of[1], (D,), jnp.float32), 0.5, 1.5).astype(jnp.bfloat16),
        "w_query": centred(streams_of[2], (D, ASKER_CHANNELS * HD), D ** -0.5, 0.125, ((0, 16),)),
        "w_key": centred(streams_of[3], (D, KVH * HD), D ** -0.5, 0.125, ((0, 16),)),
        "w_value": centred(streams_of[4], (D, KVH * HD), D ** -0.5, 0.125, ((0, 16),)),
        "b_query": centred(streams_of[5], (ASKER_CHANNELS * HD,), 0.5, 3.0),
        "b_key": centred(streams_of[6], (KVH * HD,), 0.5, 3.0),
        "b_value": centred(streams_of[7], (KVH * HD,), 0.5, 3.0),
        "cache_keys": draw_cache_keys(jax.random.fold_in(streams_of[12], 71), 0),
        "cache_values": centred(streams_of[9], (PREFIX, KVH * HD), 1.0, 6.0, ((0, 16),)),
        "block_lists": draw_block_lists(jax.random.fold_in(streams_of[12], 71), 0),
        "start_position": jax.random.randint(streams_of[11], (1,), 0, 1048576 - TOKENS + 1).astype(jnp.int32),
    }


norm_eps = 1e-06
rope_base = 10000000.0

def angle_tables(head_dim):
    half_dim = head_dim // 2
    frequency = rope_base ** (-2.0 * np.arange(half_dim) / head_dim)
    return np.stack([np.mod(frequency * 32.0 ** digit_level, 2.0 * np.pi) for digit_level in range(4)])

def rotate(values, positions):
    head_dim = values.shape[-1]
    half_dim = head_dim // 2
    tables = jnp.asarray(angle_tables(head_dim), jnp.float32)
    angles = jnp.zeros((positions.shape[0], half_dim), jnp.float32)
    remaining = positions
    for digit_level in range(4):
        digit_value = (remaining % 32).astype(jnp.float32)
        angles = angles + digit_value[:, None] * tables[digit_level][None, :]
        remaining = remaining // 32
    cosine = jnp.cos(angles)[:, None, :]
    sine_part = jnp.sin(angles)[:, None, :]
    lower_half = values[..., :half_dim]
    upper_half = values[..., half_dim:]
    return jnp.concatenate([lower_half * cosine - upper_half * sine_part, upper_half * cosine + lower_half * sine_part], axis=-1)

def reference(tokens, norm_gain, w_query, w_key, w_value, b_query, b_key, b_value, cache_keys, cache_values, block_lists, start_position):
    widened = tokens.astype(jnp.float32)
    normed = (widened * lax.rsqrt(lax.optimization_barrier(jnp.mean(widened * widened, axis=-1, keepdims=True)) + norm_eps) * norm_gain.astype(jnp.float32)).astype(jnp.bfloat16)
    query_lin = jnp.dot(normed, w_query, preferred_element_type=jnp.float32) + b_query.astype(jnp.float32)
    key_lin = jnp.dot(normed, w_key, preferred_element_type=jnp.float32) + b_key.astype(jnp.float32)
    value_lin = jnp.dot(normed, w_value, preferred_element_type=jnp.float32) + b_value.astype(jnp.float32)
    positions = start_position[0] + jnp.arange(TOKENS, dtype=jnp.int32)
    query = rotate(query_lin.reshape(TOKENS, ASKER_CHANNELS, HD), positions)
    keys_new = rotate(key_lin.reshape(TOKENS, KVH, HD), positions).reshape(TOKENS, KVH * HD)
    values_new = value_lin
    score_scale = HD ** (-0.5)
    prefix_keys = cache_keys.astype(jnp.float32).reshape(PREFIX, KVH, HD)
    prefix_values = cache_values.astype(jnp.float32).reshape(PREFIX, KVH, HD)
    block_index = jnp.arange(LEADING_TILES, dtype=jnp.int32)
    causal = jnp.arange(QBLK)[:, None] >= jnp.arange(QBLK)[None, :]

    def one_block(inputs):
        query_block, key_block, value_block, list_block = inputs
        far_scores = jnp.einsum('qkgd,pkd->kgqp', query_block, prefix_keys) * score_scale
        listed = jnp.any(list_block[:, :, None] == block_index[None, None, :], axis=1).reshape(KVH, GROUP, 1, LEADING_TILES, 1)
        far_scores = jnp.where(listed, far_scores.reshape(KVH, GROUP, QBLK, LEADING_TILES, QBLK), -jnp.inf).reshape(KVH, GROUP, QBLK, PREFIX)
        near_scores = jnp.einsum('qkgd,skd->kgqs', query_block, key_block) * score_scale
        near_scores = jnp.where(causal, near_scores, -jnp.inf)
        row_max = jnp.maximum(lax.optimization_barrier(jnp.max(far_scores, axis=-1)), lax.optimization_barrier(jnp.max(near_scores, axis=-1)))
        far_exp = jnp.exp(far_scores - row_max[..., None])
        near_exp = jnp.exp(near_scores - row_max[..., None])
        row_sum = lax.optimization_barrier(jnp.sum(far_exp, axis=-1)) + lax.optimization_barrier(jnp.sum(near_exp, axis=-1))
        mixed = jnp.einsum('kgqp,pkd->qkgd', far_exp, prefix_values)
        mixed = mixed + jnp.einsum('kgqs,skd->qkgd', near_exp, value_block)
        return (mixed / jnp.transpose(row_sum, (2, 0, 1))[..., None]).reshape(QBLK, ASKER_CHANNELS * HD)
    query_blocks = query.reshape(NQB, QBLK, KVH, GROUP, HD)
    key_blocks = keys_new.reshape(NQB, QBLK, KVH, HD)
    value_blocks = values_new.reshape(NQB, QBLK, KVH, HD)
    list_blocks = jnp.transpose(block_lists, (1, 0, 2))
    context = lax.map(one_block, (query_blocks, key_blocks, value_blocks, list_blocks)).reshape(TOKENS, ASKER_CHANNELS * HD)
    return (context, keys_new, values_new)
```

```python
import functools
import math

import jax
import jax.numpy as jnp
import numpy as np
from jax import lax
from jax.experimental import pallas as pl
from jax.experimental.pallas import tpu as pltpu
from jax.sharding import PartitionSpec as P

MESH = pl.DeviceIdType.MESH

HD = 128
GROUP = 5
QBLK = 128
SEL = 4

norm_eps = 1e-06
rope_base = 10000000.0

NX, NY, NZ = 4, 4, 8
CHUNKS = 11
AHEAD = 3
SLOTS = CHUNKS + 4


def angle_tables(head_dim):
    half_dim = head_dim // 2
    frequency = rope_base ** (-2.0 * np.arange(half_dim) / head_dim)
    tables = np.stack(
        [np.mod(frequency * 32.0**digit_level, 2.0 * np.pi) for digit_level in range(4)]
    )
    return np.concatenate([tables, tables], axis=1)


def device_of(x, y, z, core):
    return (x * 4 + (y // 2) * 2 + core, (y % 2) * NZ + z)


def kernel(
    start_ref,
    tok_ref,
    wq_ref,
    wk_ref,
    wv_ref,
    ck_ref,
    cv_ref,
    lists_ref,
    gain_ref,
    bias_ref,
    table_ref,
    ctx_ref,
    keys_ref,
    values_ref,
    wbuf,
    kvbuf,
    tokbuf,
    normed,
    cosine,
    sine,
    qbuf,
    knew,
    vnew,
    ostage,
    lvmem,
    lsmem,
    load_sem,
    z_recv,
    y_recv,
    z_send,
    y_send,
    x_recv,
    x_send,
    kv_load,
    kv_recv,
    kv_send,
    misc_sem,
    misc_send,
    out_local,
    out_send,
    out_recv,
):
    ctx = lax.axis_index("ctx")
    grp = lax.axis_index("grp")
    core = ctx % 2
    y_hi = (ctx // 2) % 2
    x = ctx // 4
    y_lo = grp // NZ
    z = grp % NZ
    y = y_hi * 2 + y_lo
    rows = tok_ref.shape[0]

    partner = device_of(x, y, z, 1 - core)
    xp = device_of((x + 1) % NX, y, z, core)
    xm = device_of((x + 3) % NX, y, z, core)
    yp = device_of(x, (y + 1) % NY, z, core)
    ym = device_of(x, (y + 3) % NY, z, core)
    zp = device_of(x, y, (z + 1) % NZ, core)
    zm = device_of(x, y, (z + 7) % NZ, core)
    ykv = device_of(x, (y + 3 + 2 * (y % 2)) % NY, z, core)

    def remote(src, dst, send_sem, recv_sem, device):
        return pltpu.make_async_remote_copy(
            src_ref=src,
            dst_ref=dst,
            send_sem=send_sem,
            recv_sem=recv_sem,
            device_id=device,
            device_id_type=MESH,
        )

    def columns(index):
        return pl.ds(pl.multiple_of(index * HD, HD), HD)

    def slot_of(i):
        return jnp.where(i == 0, 10 + x, i - 1)

    tok_load = pltpu.make_async_copy(tok_ref, tokbuf.at[0], misc_sem.at[0])
    loads = []
    for i in range(CHUNKS):
        if i == 0:
            src, dst = wq_ref.at[:, columns(core * 10 + x)], wbuf.at[10 + x, grp]
        elif i <= 4:
            ref = wk_ref if i % 2 == 1 else wv_ref
            src, dst = ref.at[:, columns(core * 2 + (i - 1) // 2)], wbuf.at[i - 1, grp]
        else:
            src, dst = wq_ref.at[:, columns(core * 10 + i - 1)], wbuf.at[i - 1, grp]
        loads.append(pltpu.make_async_copy(src, dst, load_sem.at[i]))
    kv_loads = []
    for part in range(4):
        ref = ck_ref if part < 2 else cv_ref
        kv_loads.append(
            pltpu.make_async_copy(
                ref.at[:, columns(core * 2 + part % 2)], kvbuf.at[ctx, part], kv_load.at[part]
            )
        )
    list_load = pltpu.make_async_copy(lists_ref, lsmem.at[0], misc_sem.at[3])
    for copy in kv_loads + loads[:AHEAD] + [tok_load, list_load] + loads[AHEAD:]:
        copy.start()

    barrier = pltpu.get_barrier_semaphore()
    for device in (partner, xp, xm, yp, ym, zp, zm):
        pl.semaphore_signal(barrier, inc=1, device_id=device, device_id_type=MESH)
    pl.semaphore_wait(barrier, 7)

    half = wbuf.shape[2] // 2

    def send_y(i, slot, shard):
        row = y_lo * NZ + shard
        lower, upper = wbuf.at[slot, row, 0:half], wbuf.at[slot, row, half : 2 * half]
        remote(lower, lower, y_send.at[i], y_recv.at[i], yp).start()
        remote(upper, upper, y_send.at[i], y_recv.at[i], ym).start()

    def z_copies(i, slot, step):
        from_left = wbuf.at[slot, y_lo * NZ + (z + 8 - step) % NZ]
        from_right = wbuf.at[slot, y_lo * NZ + (z + step) % NZ]
        if step == 4:
            from_left, from_right = from_left.at[0:half], from_right.at[half : 2 * half]
        return (
            remote(from_left, from_left, z_send.at[i], z_recv.at[i, step - 1], zp),
            remote(from_right, from_right, z_send.at[i], z_recv.at[i, 3 + step], zm),
        )

    def send_z(i, slot, step):
        to_right = wbuf.at[slot, y_lo * NZ + (z + 9 - step) % NZ]
        to_left = wbuf.at[slot, y_lo * NZ + (z + step - 1) % NZ]
        if step == 4:
            to_right, to_left = to_right.at[0:half], to_left.at[half : 2 * half]
        remote(to_right, to_right, z_send.at[i], z_recv.at[i, step - 1], zp).start()
        remote(to_left, to_left, z_send.at[i], z_recv.at[i, 3 + step], zm).start()

    def send_own(i, slot):
        send_z(i, slot, 1)
        send_y(i, slot, z)

    def pass_on(i, step):
        slot = slot_of(i)
        left, right = z_copies(i, slot, step)
        left.wait_recv()
        right.wait_recv()
        if step < 4:
            send_z(i, slot, step + 1)
            send_y(i, slot, (z + 8 - step) % NZ)
            send_y(i, slot, (z + step) % NZ)
        else:
            send_y(i, slot, (z + 4) % NZ)

    def wait_y(i):
        landed = wbuf.at[slot_of(i), pl.ds((1 - y_lo) * NZ, NZ)]
        remote(landed, landed, y_send.at[i], y_recv.at[i], yp).wait_recv()

    kv_parts = []
    for part in range(4):
        ref = ck_ref if part < 2 else cv_ref
        kv_parts.append(
            remote(
                ref.at[:, columns((1 - core) * 2 + part % 2)],
                kvbuf.at[ctx, part],
                kv_send.at[0],
                kv_recv.at[0],
                partner,
            )
        )

    def pair(at_x, at_y):
        return kvbuf.at[pl.ds(at_x * 4 + at_y * 2, 2)]

    left_x, right_x, far_x = (x + 3) % NX, (x + 1) % NX, (x + 2) % NX
    kv_y = remote(pair(x, y_hi), pair(x, y_hi), kv_send.at[1], kv_recv.at[1], ykv)
    kv_x = [
        remote(pair(x, y_hi), pair(x, y_hi), kv_send.at[2], kv_recv.at[2], xp),
        remote(pair(x, y_hi), pair(x, y_hi), kv_send.at[3], kv_recv.at[3], xm),
        remote(pair(x, 1 - y_hi), pair(x, 1 - y_hi), kv_send.at[4], kv_recv.at[4], xp),
        remote(pair(x, 1 - y_hi), pair(x, 1 - y_hi), kv_send.at[5], kv_recv.at[5], xm),
        remote(pair(left_x, y_hi), pair(left_x, y_hi), kv_send.at[6], kv_recv.at[6], xp),
        remote(
            pair(right_x, 1 - y_hi), pair(right_x, 1 - y_hi), kv_send.at[7], kv_recv.at[7], xm
        ),
    ]

    def shared(at_x, upper):
        return wbuf.at[10 + at_x, 8:16] if upper else wbuf.at[10 + at_x, 0:8]

    x_copies = [
        remote(shared(x, 0), shared(x, 0), x_send.at[0], x_recv.at[0], xp),
        remote(shared(x, 1), shared(x, 1), x_send.at[1], x_recv.at[1], xm),
        remote(shared(x, 1), shared(x, 1), x_send.at[2], x_recv.at[2], xp),
        remote(shared(x, 0), shared(x, 0), x_send.at[3], x_recv.at[3], xm),
        remote(shared(left_x, 0), shared(left_x, 0), x_send.at[4], x_recv.at[4], xp),
        remote(shared(right_x, 1), shared(right_x, 1), x_send.at[5], x_recv.at[5], xm),
    ]

    def norm_rows(part):
        @pl.loop(0, rows // 16)
        def _(step):
            at = pl.ds(pl.multiple_of(step * 16, 16), 16)
            wide = tokbuf[part, at, :].astype(jnp.float32)
            mean = jnp.mean(wide * wide, axis=-1, keepdims=True)
            scaled = wide * lax.rsqrt(mean + norm_eps) * gain_ref[0:1, :]
            normed[pl.ds(pl.multiple_of(part * rows + step * 16, 16), 16), :] = scaled.astype(
                jnp.bfloat16
            )

    def tables():
        lane = lax.broadcasted_iota(jnp.int32, (QBLK, HD), 1)
        sign = jnp.where(lane < HD // 2, -1.0, 1.0)

        @pl.loop(0, 2 * rows // QBLK)
        def _(step):
            of_ctx = jnp.where(step < rows // QBLK, ctx, ctx + 1 - 2 * core)
            first = (of_ctx * 16 + grp) * rows + (step % (rows // QBLK)) * QBLK
            position = start_ref[0] + first + lax.broadcasted_iota(jnp.int32, (QBLK, HD), 0)
            angle = jnp.zeros((QBLK, HD), jnp.float32)
            for level in range(4):
                digit = ((position >> (5 * level)) & 31).astype(jnp.float32)
                angle = angle + digit * table_ref[level : level + 1, :]
            turns = jnp.floor(angle * (1.0 / (2.0 * math.pi)) + 0.5)
            angle = (angle - turns * 6.28125) - turns * (2.0 * math.pi - 6.28125)
            at = pl.ds(pl.multiple_of(step * QBLK, QBLK), QBLK)
            cosine[at, :] = jnp.cos(angle)
            sine[at, :] = jnp.sin(angle) * sign

    def project(slot, bias_row):
        weights = wbuf[slot].reshape(normed.shape[1], HD)
        linear = jnp.dot(normed[...], weights, preferred_element_type=jnp.float32)
        return linear + bias_ref[pl.ds(bias_row, 1), :]

    def rope(linear):
        return linear * cosine[...] + pltpu.roll(linear, HD // 2, 1) * sine[...]

    def copy_out(slot, out_ref, column):
        own, other = ostage.at[slot, 0:rows], ostage.at[slot, rows : 2 * rows]
        target = out_ref.at[:, columns(column)]
        remote(other, target, out_send.at[0], out_recv.at[0], partner).start()
        pltpu.make_async_copy(own, target, out_local.at[0]).start()

    def key_chunk(head):
        result = rope(project(2 * head, 20 + core * 2 + head))
        knew[head] = result.astype(jnp.bfloat16)
        ostage[2 * head] = result
        copy_out(2 * head, keys_ref, core * 2 + head)

    def value_chunk(head):
        result = project(2 * head + 1, 24 + core * 2 + head)
        vnew[head] = result.astype(jnp.bfloat16)
        ostage[2 * head + 1] = result
        copy_out(2 * head + 1, values_ref, core * 2 + head)

    scale = HD**-0.5 * math.log2(math.e)
    row_at = lax.broadcasted_iota(jnp.int32, (QBLK, QBLK), 0)
    column_at = lax.broadcasted_iota(jnp.int32, (QBLK, QBLK), 1)

    def query_chunk(slot):
        local = slot % 10
        head = local // GROUP
        qbuf[...] = (rope(project(slot, core * 10 + local)) * scale).astype(jnp.bfloat16)
        for block in range(2 * rows // QBLK):
            side, part = block // (rows // QBLK), block % (rows // QBLK)
            at = slice(block * QBLK, (block + 1) * QBLK)
            entry = ((core * 10 + local) * (rows // QBLK) + part) * SEL
            keys, values, shifts = [], [], []
            for step in range(SEL):
                index = lsmem[side, (entry + step) // HD, (entry + step) % HD]
                shifts.append(jnp.where(index >= 0, 0.0, -jnp.inf))
                index = jnp.maximum(index, 0)
                keys.append(kvbuf[index, head])
                values.append(kvbuf[index, 2 + head])
            keys.append(knew[head, at, :])
            values.append(vnew[head, at, :])
            scores = lax.dot_general(
                qbuf[at, :],
                jnp.concatenate(keys, axis=0),
                (((1,), (1,)), ((), ())),
                preferred_element_type=jnp.float32,
            )
            parts = [
                scores[:, step * QBLK : (step + 1) * QBLK] + shifts[step] for step in range(SEL)
            ]
            near = scores[:, SEL * QBLK :]
            parts.append(jnp.where(row_at >= column_at, near, -jnp.inf))
            scores = jnp.concatenate(parts, axis=1)
            weights = jnp.exp2(scores - jnp.max(scores, axis=1, keepdims=True))
            total = jnp.sum(weights, axis=1, keepdims=True)
            mixed = jnp.dot(
                weights.astype(jnp.bfloat16),
                jnp.concatenate(values, axis=0),
                preferred_element_type=jnp.float32,
            )
            ostage[slot, at, :] = mixed * (1.0 / total)
        copy_out(slot, ctx_ref, core * 10 + local)

    tok_send = remote(tok_ref, tokbuf.at[1], misc_send.at[0], misc_sem.at[1], partner)
    list_send = remote(lists_ref, lvmem, misc_send.at[1], misc_sem.at[2], partner)
    for copy in kv_parts:
        copy.start()
    for i in range(AHEAD):
        loads[i].wait()
        send_own(i, 10 + x if i == 0 else i - 1)
    for copy in kv_loads:
        copy.wait()
    both = kvbuf.at[ctx + 1 - 2 * core]
    remote(both, both, kv_send.at[0], kv_recv.at[0], partner).wait_recv()
    kv_y.start()
    kv_x[0].start()
    kv_x[1].start()
    list_send.start()
    tok_send.start()
    for i in range(AHEAD, CHUNKS):
        loads[i].wait()
    tok_load.wait()
    norm_rows(0)

    @pl.loop(0, SLOTS)
    def _(now):
        @pl.when(now + AHEAD < CHUNKS)
        def _():
            send_own(now + AHEAD, now + AHEAD - 1)

        for step in (4, 3, 2, 1):

            @pl.when((now >= step - 1) & (now < CHUNKS + step - 1))
            def _():
                pass_on(now - (step - 1), step)

        @pl.when(now == 1)
        def _():
            other = pair(x, 1 - y_hi)
            remote(other, other, kv_send.at[1], kv_recv.at[1], ykv).wait_recv()
            kv_x[2].start()
            kv_x[3].start()
            here = pair(left_x, y_hi)
            remote(here, here, kv_send.at[2], kv_recv.at[2], xp).wait_recv()
            kv_x[4].start()

        @pl.when(now == 3)
        def _():
            here = pair(right_x, 1 - y_hi)
            remote(here, here, kv_send.at[5], kv_recv.at[5], xm).wait_recv()
            kv_x[5].start()

        @pl.when(now == 0)
        def _():
            tables()

        @pl.when(now == 1)
        def _():
            tok_send.wait_recv()
            norm_rows(1)

        @pl.when(now == 2)
        def _():
            list_send.wait_recv()
            list_load.wait()
            move = pltpu.make_async_copy(lvmem, lsmem.at[1], misc_sem.at[4])
            move.start()
            move.wait()

        @pl.when(now >= 4)
        def _():
            wait_y(now - 4)

        @pl.when(now == 4)
        def _():
            for copy in x_copies[:4]:
                copy.start()

        for head in range(2):

            @pl.when(now == 5 + 2 * head)
            def _():
                key_chunk(head)

            @pl.when(now == 6 + 2 * head)
            def _():
                value_chunk(head)

        @pl.when(now == 8)
        def _():
            here, there = shared(left_x, 0), shared(right_x, 1)
            remote(here, here, x_send.at[0], x_recv.at[0], xp).wait_recv()
            x_copies[4].start()
            remote(there, there, x_send.at[1], x_recv.at[1], xm).wait_recv()
            x_copies[5].start()
            for landed, sem in (
                (pair(right_x, y_hi), 3),
                (pair(left_x, 1 - y_hi), 4),
                (pair(far_x, y_hi), 6),
                (pair(far_x, 1 - y_hi), 7),
            ):
                remote(landed, landed, kv_send.at[sem], kv_recv.at[sem], xp).wait_recv()

        @pl.when(now == 12)
        def _():
            here = shared(left_x, 1)
            remote(here, here, x_send.at[2], x_recv.at[2], xp).wait_recv()

        @pl.when(now == 13)
        def _():
            here = shared(right_x, 0)
            remote(here, here, x_send.at[3], x_recv.at[3], xm).wait_recv()

        @pl.when(now == 14)
        def _():
            here, there = shared(far_x, 0), shared(far_x, 1)
            remote(here, here, x_send.at[4], x_recv.at[4], xp).wait_recv()
            remote(there, there, x_send.at[5], x_recv.at[5], xm).wait_recv()

        extra = jnp.where(now == 9, 0, jnp.where(now == 12, 3, jnp.where(now == 13, 1, 2)))
        jobs = jnp.where(now >= 9, jnp.where((now == 10) | (now == 11), 1, 2), 0)

        def job(which, carry):
            query_chunk(jnp.where(which == 0, now - 5, 10 + (x + extra) % NX))
            return carry

        lax.fori_loop(0, jobs, job, 0)

    @pl.loop(0, CHUNKS)
    def _(i):
        sent = wbuf.at[0, 0:7]
        pltpu.make_async_copy(sent, sent, z_send.at[i]).wait()
        sent = wbuf.at[0, 0:8]
        pltpu.make_async_copy(sent, sent, y_send.at[i]).wait()

    for copy in x_copies:
        copy.wait_send()
    pltpu.make_async_copy(kvbuf.at[0], kvbuf.at[0], kv_send.at[0]).wait()
    kv_y.wait_send()
    for copy in kv_x:
        copy.wait_send()
    tok_send.wait_send()
    list_send.wait_send()
    written = ostage.at[0:7]
    pltpu.make_async_copy(written, written, out_local.at[0]).wait()
    pltpu.make_async_copy(written, written, out_send.at[0]).wait()
    pltpu.make_async_copy(written, written, out_recv.at[0]).wait()


def on_device(
    tokens,
    norm_gain,
    w_query,
    w_key,
    w_value,
    b_query,
    b_key,
    b_value,
    cache_keys,
    cache_values,
    block_lists,
    start_position,
):
    rows, features = tokens.shape
    shard = w_query.shape[0]
    bias = jnp.concatenate([b_query, b_key, b_value]).astype(jnp.float32).reshape(28, HD)
    bias = jnp.pad(bias, ((0, 4), (0, 0)))
    gain = jnp.broadcast_to(norm_gain.astype(jnp.float32)[None, :], (8, features))
    lists = jnp.pad(block_lists.reshape(-1), (0, 1024 - block_lists.size)).reshape(8, HD)
    table = jnp.asarray(np.pad(angle_tables(HD), ((0, 4), (0, 0))), jnp.float32)
    hbm = pl.BlockSpec(memory_space=pl.ANY)
    vmem = pl.BlockSpec(memory_space=pltpu.VMEM)
    smem = pl.BlockSpec(memory_space=pltpu.SMEM)
    dma = pltpu.SemaphoreType.DMA
    return pl.pallas_call(
        kernel,
        out_shape=(
            jax.ShapeDtypeStruct((rows, 20 * HD), jnp.float32),
            jax.ShapeDtypeStruct((rows, 4 * HD), jnp.float32),
            jax.ShapeDtypeStruct((rows, 4 * HD), jnp.float32),
        ),
        in_specs=[smem] + [hbm] * 6 + [vmem] * 4,
        out_specs=[hbm] * 3,
        scratch_shapes=[
            pltpu.VMEM((14, 16, shard, HD), jnp.bfloat16),
            pltpu.VMEM((16, 4, QBLK, HD), jnp.bfloat16),
            pltpu.VMEM((2, rows, features), jnp.bfloat16),
            pltpu.VMEM((2 * rows, features), jnp.bfloat16),
            pltpu.VMEM((2 * rows, HD), jnp.float32),
            pltpu.VMEM((2 * rows, HD), jnp.float32),
            pltpu.VMEM((2 * rows, HD), jnp.bfloat16),
            pltpu.VMEM((2, 2 * rows, HD), jnp.bfloat16),
            pltpu.VMEM((2, 2 * rows, HD), jnp.bfloat16),
            pltpu.VMEM((14, 2 * rows, HD), jnp.float32),
            pltpu.VMEM((8, HD), jnp.int32),
            pltpu.SMEM((2, 8, HD), jnp.int32),
            dma((CHUNKS,)),
            dma((CHUNKS, 8)),
            dma((CHUNKS,)),
            dma((CHUNKS,)),
            dma((CHUNKS,)),
            dma((6,)),
            dma((6,)),
            dma((4,)),
            dma((8,)),
            dma((8,)),
            dma((5,)),
            dma((2,)),
            dma((1,)),
            dma((1,)),
            dma((1,)),
        ],
        compiler_params=pltpu.CompilerParams(
            collective_id=0, has_side_effects=True, vmem_limit_bytes=48 << 20
        ),
        name="gather_attend",
    )(
        start_position,
        tokens,
        w_query,
        w_key,
        w_value,
        cache_keys,
        cache_values,
        lists,
        gain,
        bias,
        table,
    )


def solution(mesh):
    in_specs = (
        P(("ctx", "grp"), None),
        P(),
        P("grp", None),
        P("grp", None),
        P("grp", None),
        P(),
        P(),
        P(),
        P("ctx", None),
        P("ctx", None),
        P(None, ("ctx", "grp"), None),
        P(),
    )
    out_specs = (P(("ctx", "grp"), None), P(("ctx", "grp"), None), P(("ctx", "grp"), None))
    return jax.shard_map(
        on_device, mesh=mesh, in_specs=in_specs, out_specs=out_specs, check_vma=False
    )
```

```python
import functools
import math

import jax
import jax.numpy as jnp
import numpy as np
from jax import lax
from jax.experimental import pallas as pl
from jax.experimental.pallas import tpu as pltpu
from jax.sharding import PartitionSpec as P

MESH = pl.DeviceIdType.MESH

HD = 128
GROUP = 5
QBLK = 128
SEL = 4

norm_eps = 1e-06
rope_base = 10000000.0

NX, NY, NZ = 4, 4, 8
CHUNKS = 11
PLACE = (None, 0, 1, 4, 2, 3, 5, 6, 7, 8, 9)

Y_FIRST = (8,)
SCHEDULE = (
    ((
        ("own", 0), ("own", 1),
    ), ("N0",)),
    ((
        ("own", 2), ("own", 3),
    ), ("T",)),
    ((
        ("kv0",), ("own", 4),
    ), ("N1",)),
    ((
        ("z", 0, 1, 0), ("z", 1, 1, 0), ("z", 2, 1, 0), ("z", 3, 1, 0), ("z", 4, 1, 0),
        ("z", 0, 2, 0), ("z", 1, 2, 0), ("z", 2, 2, 0), ("z", 3, 2, 0), ("kv1",), ("kv2",),
        ("z", 4, 2, 0), ("z", 0, 3, 0), ("z", 1, 3, 0), ("own", 5), ("z", 2, 3, 0),
        ("z", 3, 3, 0), ("own", 6), ("z", 4, 3, 0), ("z", 0, 4, 0), ("z", 1, 4, 0), ("own", 7),
        ("z", 5, 1, 0), ("z", 2, 4, 0), ("z", 3, 4, 0), ("own", 8), ("kv3",), ("z", 6, 1, 0),
        ("z", 4, 4, 0), ("own", 9), ("z", 7, 1, 0), ("z", 5, 2, 0), ("z", 8, 1, 0),
        ("z", 6, 2, 0), ("b0",), ("z", 9, 1, 0), ("z", 7, 2, 0), ("z", 5, 3, 0), ("y", 1),
        ("y", 2),
    ), ("K", 0)),
    ((
        ("own", 10), ("z", 6, 3, 0), ("yf", 8), ("z", 8, 2, 0), ("y", 3), ("kvw",),
    ), ("P", 0)),
    ((
        ("z", 7, 3, 0), ("z", 5, 4, 0), ("z", 9, 2, 0),
    ), ("A", 0)),
    ((
        ("z", 10, 1, 0),
    ), ("A", 1)),
    ((
        ("z", 6, 4, 0), ("z", 8, 1, 1), ("z", 8, 3, 0), ("z", 7, 4, 0), ("b1",), ("z", 9, 3, 0),
        ("z", 10, 2, 0), ("y", 4), ("y", 5),
    ), ("K", 1)),
    ((
        ("z", 8, 2, 1), ("z", 8, 4, 0), ("z", 9, 4, 0), ("y", 6), ("y", 7),
    ), ("P", 1)),
    ((
        ("z", 10, 3, 0),
    ), ("A", 2)),
    ((

    ), ("A", 3)),
    ((
        ("z", 8, 3, 1), ("b2",),
    ), ("P", 3)),
    ((
        ("z", 10, 4, 0),
    ), ("A", 6)),
    ((

    ), ("A", 7)),
    ((
        ("z", 8, 4, 1), ("y", 8), ("y", 9),
    ), ("P", 2)),
    ((

    ), ("A", 4)),
    ((

    ), ("A", 5)),
    ((
        ("y", 10), ("b3",),
    ), ("P", 4)),
    ((

    ), ("A", 8)),
    ((

    ), ("A", 9)),
)
AHEAD = sum(op[0] == "own" for op in SCHEDULE[0][0])


def angle_tables(head_dim):
    half_dim = head_dim // 2
    frequency = rope_base ** (-2.0 * np.arange(half_dim) / head_dim)
    tables = np.stack(
        [np.mod(frequency * 32.0**digit_level, 2.0 * np.pi) for digit_level in range(4)]
    )
    return np.concatenate([tables, tables], axis=1)


def device_of(x, y, z, core):
    return (x * 4 + (y // 2) * 2 + core, (y % 2) * NZ + z)


def kernel(
    start_ref,
    tok_ref,
    wq_ref,
    wk_ref,
    wv_ref,
    ck_ref,
    cv_ref,
    lists_ref,
    prep_ref,
    table_hbm,
    ctx_ref,
    keys_ref,
    values_ref,
    wbuf,
    kvbuf,
    tokbuf,
    normed,
    cosine,
    sine,
    qbuf,
    knew,
    vnew,
    ostage,
    gain_ref,
    table_ref,
    lvmem,
    lsmem,
    load_sem,
    z_recv,
    z_recv_across,
    y_recv,
    z_send,
    y_send,
    x_recv,
    x_send,
    kv_load,
    kv_recv,
    kv_send,
    misc_sem,
    misc_send,
    out_local,
    out_send,
    out_recv,
):
    ctx = lax.axis_index("ctx")
    grp = lax.axis_index("grp")
    core = ctx % 2
    y_hi = (ctx // 2) % 2
    x = ctx // 4
    y_lo = grp // NZ
    z = grp % NZ
    y = y_hi * 2 + y_lo
    rows = tok_ref.shape[0]

    partner = device_of(x, y, z, 1 - core)
    xp = device_of((x + 1) % NX, y, z, core)
    xm = device_of((x + 3) % NX, y, z, core)
    yp = device_of(x, (y + 1) % NY, z, core)
    ym = device_of(x, (y + 3) % NY, z, core)
    zp = device_of(x, y, (z + 1) % NZ, core)
    zm = device_of(x, y, (z + 7) % NZ, core)
    ykv = device_of(x, (y + 3 + 2 * (y % 2)) % NY, z, core)
    yother = device_of(x, (y + 1 + 2 * (y % 2)) % NY, z, core)

    def remote(src, dst, send_sem, recv_sem, device):
        return pltpu.make_async_remote_copy(
            src_ref=src,
            dst_ref=dst,
            send_sem=send_sem,
            recv_sem=recv_sem,
            device_id=device,
            device_id_type=MESH,
        )

    def columns(index):
        return pl.ds(pl.multiple_of(index * HD, HD), HD)

    def slot_of(i):
        return 10 + x if i == 0 else PLACE[i]

    tok_load = pltpu.make_async_copy(tok_ref, tokbuf.at[0], misc_sem.at[0])
    loads = []
    for i in range(CHUNKS):
        place = PLACE[i]
        if i == 0:
            src = wq_ref.at[:, columns(core * 10 + x)]
        elif place < 4:
            ref = wk_ref if place % 2 == 0 else wv_ref
            src = ref.at[:, columns(core * 2 + place // 2)]
        else:
            src = wq_ref.at[:, columns(core * 10 + place)]
        loads.append(pltpu.make_async_copy(src, wbuf.at[slot_of(i), grp], load_sem.at[i]))
    kv_loads = []
    for part in range(4):
        ref = ck_ref if part < 2 else cv_ref
        kv_loads.append(
            pltpu.make_async_copy(
                ref.at[:, columns(core * 2 + part % 2)], kvbuf.at[ctx, part], kv_load.at[part]
            )
        )
    list_load = pltpu.make_async_copy(lists_ref, lsmem.at[0], misc_sem.at[3])
    table_load = pltpu.make_async_copy(table_hbm, table_ref, misc_sem.at[5])
    for copy in kv_loads + loads[:AHEAD] + [tok_load, list_load, table_load] + loads[AHEAD:]:
        copy.start()

    barrier = pltpu.get_barrier_semaphore()
    for device in (partner, xp, xm, yp, ym, zp, zm):
        pl.semaphore_signal(barrier, inc=1, device_id=device, device_id_type=MESH)
    pl.semaphore_wait(barrier, 7)

    shard_rows = wbuf.shape[2]
    half = shard_rows // 2

    def send_y(i, slot, shard, distance):
        row = y_lo * NZ + shard
        cut = half - 16 if distance <= 1 else half
        lower, upper = wbuf.at[slot, row, 0:cut], wbuf.at[slot, row, cut:shard_rows]
        remote(lower, lower, y_send.at[i], y_recv.at[i], ykv).start()
        remote(upper, upper, y_send.at[i], y_recv.at[i], yother).start()

    def send_z(i, slot, distance, line, wait=False):
        base = (y_lo if line == 0 else 1 - y_lo) * NZ
        back = 0 if wait else 1
        rightward = wbuf.at[slot, base + (z + 8 - distance + back) % NZ]
        leftward = wbuf.at[slot, base + (z + distance - back) % NZ]
        if distance == 4:
            rightward, leftward = rightward.at[0:half], leftward.at[half:shard_rows]
        recv = [
            z_recv.at[i, n] if line == 0 else z_recv_across.at[n]
            for n in (distance - 1, 3 + distance)
        ]
        copies = (
            remote(rightward, rightward, z_send.at[i], recv[0], zp),
            remote(leftward, leftward, z_send.at[i], recv[1], zm),
        )
        for copy in copies:
            if wait:
                copy.wait_recv()
            else:
                copy.start()

    def send_own(i):
        slot = slot_of(i)
        loads[i].wait()
        send_z(i, slot, 1, 0)
        send_y(i, slot, z, 0)

    def pass_on(i, distance, line):
        slot = slot_of(i)
        send_z(i, slot, distance, line, wait=True)
        if distance < 4:
            send_z(i, slot, distance + 1, line)
        if i in Y_FIRST:
            return
        send_y(i, slot, (z + 8 - distance) % NZ, distance)
        if distance < 4:
            send_y(i, slot, (z + distance) % NZ, distance)

    def send_across(i):
        slot = slot_of(i)
        landed = wbuf.at[slot, (1 - y_lo) * NZ + z]
        remote(landed, landed, y_send.at[i], y_recv.at[i], ykv).wait_recv()
        send_z(i, slot, 1, 1)

    def wait_y(i):
        if i in Y_FIRST:
            return
        landed = wbuf.at[slot_of(i), pl.ds((1 - y_lo) * NZ, NZ)]
        remote(landed, landed, y_send.at[i], y_recv.at[i], ykv).wait_recv()

    kv_parts = []
    for part in range(4):
        ref = ck_ref if part < 2 else cv_ref
        kv_parts.append(
            remote(
                ref.at[:, columns((1 - core) * 2 + part % 2)],
                kvbuf.at[ctx, part],
                kv_send.at[0],
                kv_recv.at[0],
                partner,
            )
        )

    def pair(at_x, at_y):
        return kvbuf.at[pl.ds(at_x * 4 + at_y * 2, 2)]

    left_x, right_x, far_x = (x + 3) % NX, (x + 1) % NX, (x + 2) % NX
    kv_y = remote(pair(x, y_hi), pair(x, y_hi), kv_send.at[1], kv_recv.at[1], ykv)
    kv_x = [
        remote(pair(x, y_hi), pair(x, y_hi), kv_send.at[2], kv_recv.at[2], xp),
        remote(pair(x, y_hi), pair(x, y_hi), kv_send.at[3], kv_recv.at[3], xm),
        remote(pair(x, 1 - y_hi), pair(x, 1 - y_hi), kv_send.at[4], kv_recv.at[4], xp),
        remote(pair(x, 1 - y_hi), pair(x, 1 - y_hi), kv_send.at[5], kv_recv.at[5], xm),
        remote(pair(left_x, y_hi), pair(left_x, y_hi), kv_send.at[6], kv_recv.at[6], xp),
        remote(
            pair(right_x, 1 - y_hi), pair(right_x, 1 - y_hi), kv_send.at[7], kv_recv.at[7], xm
        ),
    ]

    def shared(at_x, upper):
        return wbuf.at[10 + at_x, 8:16] if upper else wbuf.at[10 + at_x, 0:8]

    x_copies = [
        remote(shared(x, 0), shared(x, 0), x_send.at[0], x_recv.at[0], xp),
        remote(shared(x, 1), shared(x, 1), x_send.at[1], x_recv.at[1], xm),
        remote(shared(x, 1), shared(x, 1), x_send.at[2], x_recv.at[2], xp),
        remote(shared(x, 0), shared(x, 0), x_send.at[3], x_recv.at[3], xm),
        remote(shared(left_x, 0), shared(left_x, 0), x_send.at[4], x_recv.at[4], xp),
        remote(shared(right_x, 1), shared(right_x, 1), x_send.at[5], x_recv.at[5], xm),
    ]

    def norm_rows(part):
        @pl.loop(0, rows // 64)
        def _(step):
            at = pl.ds(pl.multiple_of(step * 64, 64), 64)
            wide = tokbuf[part, at, :].astype(jnp.float32)
            mean = jnp.mean(wide * wide, axis=-1, keepdims=True)
            scaled = wide * lax.rsqrt(mean + norm_eps) * gain_ref[0:1, :]
            normed[pl.ds(pl.multiple_of(part * rows + step * 64, 64), 64), :] = scaled.astype(
                jnp.bfloat16
            )

    def tables():
        lane = lax.broadcasted_iota(jnp.int32, (QBLK, HD), 1)
        sign = jnp.where(lane < HD // 2, -1.0, 1.0)

        @pl.loop(0, 2 * rows // QBLK)
        def _(step):
            of_ctx = jnp.where(step < rows // QBLK, ctx, ctx + 1 - 2 * core)
            first = (of_ctx * 16 + grp) * rows + (step % (rows // QBLK)) * QBLK
            position = start_ref[0] + first + lax.broadcasted_iota(jnp.int32, (QBLK, HD), 0)
            angle = jnp.zeros((QBLK, HD), jnp.float32)
            for level in range(4):
                digit = ((position >> (5 * level)) & 31).astype(jnp.float32)
                angle = angle + digit * table_ref[level : level + 1, :]
            turns = jnp.floor(angle * (1.0 / (2.0 * math.pi)) + 0.5)
            angle = (angle - turns * 6.28125) - turns * (2.0 * math.pi - 6.28125)
            at = pl.ds(pl.multiple_of(step * QBLK, QBLK), QBLK)
            cosine[at, :] = jnp.cos(angle)
            sine[at, :] = jnp.sin(angle) * sign

    def project(slots, bias_rows):
        weights = [wbuf[slot].reshape(normed.shape[1], HD) for slot in slots]
        linear = jnp.dot(
            normed[...], jnp.concatenate(weights, axis=1), preferred_element_type=jnp.float32
        )
        return [
            linear[:, n * HD : (n + 1) * HD] + prep_ref[pl.ds(20 + row, 1), :]
            for n, row in enumerate(bias_rows)
        ]

    def rope(linear):
        return linear * cosine[...] + pltpu.roll(linear, HD // 2, 1) * sine[...]

    def copy_out(slot, out_ref, column):
        own, other = ostage.at[slot, 0:rows], ostage.at[slot, rows : 2 * rows]
        target = out_ref.at[:, columns(column)]
        remote(other, target, out_send.at[0], out_recv.at[0], partner).start()
        pltpu.make_async_copy(own, target, out_local.at[0]).start()

    def key_value_chunks(head):
        global_head = core * 2 + head
        linear_key, linear_value = project(
            (2 * head, 2 * head + 1), (20 + global_head, 24 + global_head)
        )
        key = rope(linear_key)
        knew[head] = key.astype(jnp.bfloat16)
        ostage[2 * head] = key
        copy_out(2 * head, keys_ref, global_head)
        vnew[head] = linear_value.astype(jnp.bfloat16)
        ostage[2 * head + 1] = linear_value
        copy_out(2 * head + 1, values_ref, global_head)

    scale = HD**-0.5 * math.log2(math.e)
    row_at = lax.broadcasted_iota(jnp.int32, (QBLK, QBLK), 0)
    column_at = lax.broadcasted_iota(jnp.int32, (QBLK, QBLK), 1)
    blocks = rows // QBLK

    def attend(n, slot):
        local = slot % 10
        head = local // GROUP
        scores, values = [], []
        for block in range(2 * blocks):
            at = slice(block * QBLK, (block + 1) * QBLK)
            keys, shifts = [], []
            values.append([])
            for step in range(SEL):
                index = lsmem[block // blocks, block % blocks, step, core * 10 + local]
                shifts.append(jnp.where(index >= 0, 0.0, -jnp.inf))
                index = jnp.maximum(index, 0)
                keys.append(kvbuf[index, head])
                values[-1].append(kvbuf[index, 2 + head])
            keys.append(knew[head, at, :])
            values[-1].append(vnew[head, at, :])
            all_keys = lax.dot_general(
                qbuf[n, at, :],
                jnp.concatenate(keys, axis=0),
                (((1,), (1,)), ((), ())),
                preferred_element_type=jnp.float32,
            )
            parts = [
                all_keys[:, step * QBLK : (step + 1) * QBLK] + shifts[step] for step in range(SEL)
            ]
            near = all_keys[:, SEL * QBLK :]
            scores.append(parts + [jnp.where(row_at >= column_at, near, -jnp.inf)])
        largest = [
            jnp.max(functools.reduce(jnp.maximum, parts), axis=1, keepdims=True)
            for parts in scores
        ]
        for block in range(2 * blocks):
            at = slice(block * QBLK, (block + 1) * QBLK)
            weights = [jnp.exp2(part - largest[block]) for part in scores[block]]
            total = jnp.sum(functools.reduce(jnp.add, weights), axis=1, keepdims=True)
            mixed = jnp.dot(
                jnp.concatenate([part.astype(jnp.bfloat16) for part in weights], axis=1),
                jnp.concatenate(values[block], axis=0),
                preferred_element_type=jnp.float32,
            )
            ostage[slot, at, :] = mixed * (1.0 / total)
        copy_out(slot, ctx_ref, core * 10 + local)

    def query_chunks(first, second):
        heads = (core * 10 + first % 10, core * 10 + second % 10)
        linear = project((first, second), heads)
        for n in range(2):
            qbuf[n] = (rope(linear[n]) * scale).astype(jnp.bfloat16)

    tok_send = remote(tok_ref, tokbuf.at[1], misc_send.at[0], misc_sem.at[1], partner)
    list_send = remote(lists_ref, lvmem, misc_send.at[1], misc_sem.at[2], partner)

    def kv_wait(landed, number):
        remote(landed, landed, kv_send.at[number], kv_recv.at[number], xp).wait_recv()

    def shared_wait(landed, number):
        remote(landed, landed, x_send.at[number], x_recv.at[number], xp).wait_recv()

    def run(op):
        kind, at = op[0], op[1:]
        if kind == "own":
            send_own(*at)
        elif kind == "z":
            pass_on(*at)
        elif kind == "yf":
            send_across(*at)
        elif kind == "y":
            wait_y(*at)
        elif kind == "kv0":
            for copy in kv_loads:
                copy.wait()
            kv_wait(kvbuf.at[ctx + 1 - 2 * core], 0)
            kv_y.start()
            kv_x[0].start()
            kv_x[1].start()
        elif kind == "kv1":
            kv_wait(pair(x, 1 - y_hi), 1)
            kv_x[2].start()
            kv_x[3].start()
        elif kind == "kv2":
            kv_wait(pair(left_x, y_hi), 2)
            kv_x[4].start()
        elif kind == "kv3":
            kv_wait(pair(right_x, 1 - y_hi), 5)
            kv_x[5].start()
        elif kind == "kvw":
            kv_wait(pair(right_x, y_hi), 3)
            kv_wait(pair(left_x, 1 - y_hi), 4)
            kv_wait(pair(far_x, y_hi), 6)
            kv_wait(pair(far_x, 1 - y_hi), 7)
        elif kind == "b0":
            wait_y(0)
            for copy in x_copies[:4]:
                copy.start()
        elif kind == "b1":
            shared_wait(shared(left_x, 0), 0)
            shared_wait(shared(right_x, 1), 1)
            x_copies[4].start()
            x_copies[5].start()
        elif kind == "b2":
            shared_wait(shared(left_x, 1), 2)
            shared_wait(shared(right_x, 0), 3)
        elif kind == "b3":
            shared_wait(shared(far_x, 0), 4)
            shared_wait(shared(far_x, 1), 5)

    for copy in kv_parts:
        copy.start()
    for op in SCHEDULE[0][0][:AHEAD]:
        run(op)
    list_send.start()
    tok_send.start()
    table_load.wait()
    for step in range(gain_ref.shape[1] // HD):
        gain_ref[0:1, step * HD : (step + 1) * HD] = prep_ref[step : step + 1, :]

    pairs = (
        (10 + x, 4),
        (5, 6),
        (7, 8),
        (10 + left_x, 10 + right_x),
        (9, 10 + far_x),
    )
    units = [unit for _, unit in SCHEDULE]

    @pl.loop(0, len(SCHEDULE))
    def _(now):
        for number, (ops, _unused) in enumerate(SCHEDULE):
            rest = ops[AHEAD:] if number == 0 else ops
            if rest:

                @pl.when(now == number)
                def _():
                    for op in rest:
                        run(op)

        def on(kind):
            places = [n for n, unit in enumerate(units) if unit[0] == kind]
            condition = functools.reduce(jnp.logical_or, [now == n for n in places])

            def pick(values):
                value = values[units[places[-1]][1]]
                for n in places[:-1]:
                    value = jnp.where(now == n, values[units[n][1]], value)
                return value

            return condition, pick

        @pl.when(on("N0")[0])
        def _():
            tok_load.wait()
            norm_rows(0)

        @pl.when(on("T")[0])
        def _():
            tables()

        @pl.when(on("N1")[0])
        def _():
            tok_send.wait_recv()
            norm_rows(1)
            list_send.wait_recv()
            list_load.wait()
            move = pltpu.make_async_copy(lvmem, lsmem.at[1], misc_sem.at[4])
            move.start()
            move.wait()

        condition, pick_pair = on("K")

        @pl.when(condition)
        def _():
            key_value_chunks(pick_pair((0, 1)))

        condition, pick_query = on("P")

        @pl.when(condition)
        def _():
            query_chunks(
                pick_query([first for first, _ in pairs]),
                pick_query([second for _, second in pairs]),
            )

        condition, pick_head = on("A")

        @pl.when(condition)
        def _():
            flat = [slot for both in pairs for slot in both]
            attend(pick_head([n % 2 for n in range(len(flat))]), pick_head(flat))

    for i in range(CHUNKS):
        sent = wbuf.at[0, 0:14] if i in Y_FIRST else wbuf.at[0, 0:7]
        pltpu.make_async_copy(sent, sent, z_send.at[i]).wait()
        sent = wbuf.at[0, 0] if i in Y_FIRST else wbuf.at[0, 0:8]
        pltpu.make_async_copy(sent, sent, y_send.at[i]).wait()

    for copy in x_copies:
        copy.wait_send()
    pltpu.make_async_copy(kvbuf.at[0], kvbuf.at[0], kv_send.at[0]).wait()
    kv_y.wait_send()
    for copy in kv_x:
        copy.wait_send()
    tok_send.wait_send()
    list_send.wait_send()
    written = ostage.at[0:7]
    pltpu.make_async_copy(written, written, out_local.at[0]).wait()
    pltpu.make_async_copy(written, written, out_send.at[0]).wait()
    pltpu.make_async_copy(written, written, out_recv.at[0]).wait()


def on_device(
    tokens,
    norm_gain,
    w_query,
    w_key,
    w_value,
    b_query,
    b_key,
    b_value,
    cache_keys,
    cache_values,
    block_lists,
    start_position,
):
    rows, features = tokens.shape
    shard = w_query.shape[0]
    prep = jnp.concatenate([norm_gain, b_query, b_key, b_value]).reshape(48, HD)
    prep = prep.astype(jnp.float32)
    lists = jnp.transpose(block_lists, (1, 2, 0))
    table = jnp.asarray(np.pad(angle_tables(HD), ((0, 4), (0, 0))), jnp.float32)
    hbm = pl.BlockSpec(memory_space=pltpu.HBM)
    vmem = pl.BlockSpec(memory_space=pltpu.VMEM)
    smem = pl.BlockSpec(memory_space=pltpu.SMEM)
    dma = pltpu.SemaphoreType.DMA
    return pl.pallas_call(
        kernel,
        out_shape=(
            jax.ShapeDtypeStruct((rows, 20 * HD), jnp.float32),
            jax.ShapeDtypeStruct((rows, 4 * HD), jnp.float32),
            jax.ShapeDtypeStruct((rows, 4 * HD), jnp.float32),
        ),
        in_specs=[smem] + [hbm] * 7 + [vmem] + [hbm],
        out_specs=[hbm] * 3,
        scratch_shapes=[
            pltpu.VMEM((14, 16, shard, HD), jnp.bfloat16),
            pltpu.VMEM((16, 4, QBLK, HD), jnp.bfloat16),
            pltpu.VMEM((2, rows, features), jnp.bfloat16),
            pltpu.VMEM((2 * rows, features), jnp.bfloat16),
            pltpu.VMEM((2 * rows, HD), jnp.float32),
            pltpu.VMEM((2 * rows, HD), jnp.float32),
            pltpu.VMEM((2, 2 * rows, HD), jnp.bfloat16),
            pltpu.VMEM((2, 2 * rows, HD), jnp.bfloat16),
            pltpu.VMEM((2, 2 * rows, HD), jnp.bfloat16),
            pltpu.VMEM((14, 2 * rows, HD), jnp.float32),
            pltpu.VMEM((8, features), jnp.float32),
            pltpu.VMEM((8, HD), jnp.float32),
            pltpu.VMEM(lists.shape, jnp.int32),
            pltpu.SMEM((2,) + lists.shape, jnp.int32),
            dma((CHUNKS,)),
            dma((CHUNKS, 8)),
            dma((8,)),
            dma((CHUNKS,)),
            dma((CHUNKS,)),
            dma((CHUNKS,)),
            dma((6,)),
            dma((6,)),
            dma((4,)),
            dma((8,)),
            dma((8,)),
            dma((6,)),
            dma((2,)),
            dma((1,)),
            dma((1,)),
            dma((1,)),
        ],
        compiler_params=pltpu.CompilerParams(
            collective_id=0, has_side_effects=True, vmem_limit_bytes=58 << 20
        ),
        name="gather_attend",
    )(
        start_position,
        tokens,
        w_query,
        w_key,
        w_value,
        cache_keys,
        cache_values,
        lists,
        prep,
        table,
    )


def solution(mesh):
    in_specs = (
        P(("ctx", "grp"), None),
        P(),
        P("grp", None),
        P("grp", None),
        P("grp", None),
        P(),
        P(),
        P(),
        P("ctx", None),
        P("ctx", None),
        P(None, ("ctx", "grp"), None),
        P(),
    )
    out_specs = (P(("ctx", "grp"), None), P(("ctx", "grp"), None), P(("ctx", "grp"), None))
    return jax.shard_map(
        on_device, mesh=mesh, in_specs=in_specs, out_specs=out_specs, check_vma=False
    )
```

```python
import functools
import math

import jax
import jax.numpy as jnp
import numpy as np
from jax import lax
from jax.experimental import pallas as pl
from jax.experimental.pallas import tpu as pltpu
from jax.sharding import PartitionSpec as P

MESH = pl.DeviceIdType.MESH

HD = 128
GROUP = 5
QBLK = 128
SEL = 4

norm_eps = 1e-06
rope_base = 10000000.0

NX, NY, NZ = 4, 4, 8
CHUNKS = 11
PLACE = (None, 0, 1, 4, 2, 3, 5, 6, 7, 8, 9)

Y_FIRST = (8,)
SCHEDULE = (
    ((
        ("own", 0), ("own", 1),
    ), ("N0",)),
    ((
        ("own", 2), ("own", 3),
    ), ("T",)),
    ((
        ("kv0",), ("own", 4),
    ), ("N1",)),
    ((
        ("z", 0, 1, 0), ("z", 1, 1, 0), ("z", 2, 1, 0), ("z", 3, 1, 0), ("z", 4, 1, 0),
        ("z", 0, 2, 0), ("z", 1, 2, 0), ("z", 2, 2, 0), ("z", 3, 2, 0), ("kv1",), ("kv2",),
        ("z", 4, 2, 0), ("z", 0, 3, 0), ("z", 1, 3, 0), ("own", 5), ("z", 2, 3, 0),
        ("z", 3, 3, 0), ("own", 6), ("z", 4, 3, 0), ("z", 0, 4, 0), ("z", 1, 4, 0), ("own", 7),
        ("z", 5, 1, 0), ("z", 2, 4, 0), ("z", 3, 4, 0), ("own", 8), ("kv3",), ("z", 6, 1, 0),
        ("z", 4, 4, 0), ("own", 9), ("z", 7, 1, 0), ("z", 5, 2, 0), ("z", 8, 1, 0),
        ("z", 6, 2, 0), ("b0",), ("z", 9, 1, 0), ("z", 7, 2, 0), ("z", 5, 3, 0), ("y", 1),
        ("y", 2),
    ), ("K", 0)),
    ((
        ("own", 10), ("z", 6, 3, 0), ("yf", 8), ("z", 8, 2, 0), ("y", 3), ("kvw",),
    ), ("P", 0)),
    ((
        ("z", 7, 3, 0), ("z", 5, 4, 0), ("z", 9, 2, 0),
    ), ("A", 0)),
    ((
        ("z", 10, 1, 0),
    ), ("A", 1)),
    ((
        ("z", 6, 4, 0), ("z", 8, 1, 1), ("z", 8, 3, 0), ("z", 7, 4, 0), ("b1",), ("z", 9, 3, 0),
        ("z", 10, 2, 0), ("y", 4), ("y", 5),
    ), ("K", 1)),
    ((
        ("z", 8, 2, 1), ("z", 8, 4, 0), ("z", 9, 4, 0), ("y", 6), ("y", 7),
    ), ("P", 1)),
    ((
        ("z", 10, 3, 0),
    ), ("A", 2)),
    ((

    ), ("A", 3)),
    ((
        ("z", 8, 3, 1), ("b2",),
    ), ("P", 3)),
    ((
        ("z", 10, 4, 0),
    ), ("A", 6)),
    ((

    ), ("A", 7)),
    ((
        ("z", 8, 4, 1), ("y", 8), ("y", 9),
    ), ("P", 2)),
    ((

    ), ("A", 4)),
    ((

    ), ("A", 5)),
    ((
        ("y", 10), ("b3",),
    ), ("P", 4)),
    ((

    ), ("A", 8)),
    ((

    ), ("A", 9)),
)
AHEAD = sum(op[0] == "own" for op in SCHEDULE[0][0])


def angle_tables(head_dim):
    half_dim = head_dim // 2
    frequency = rope_base ** (-2.0 * np.arange(half_dim) / head_dim)
    tables = np.stack(
        [np.mod(frequency * 32.0**digit_level, 2.0 * np.pi) for digit_level in range(4)]
    )
    return np.concatenate([tables, tables], axis=1)


def device_of(x, y, z, core):
    return (x * 4 + (y // 2) * 2 + core, (y % 2) * NZ + z)


def kernel(
    start_ref,
    tok_ref,
    wq_ref,
    wk_ref,
    wv_ref,
    ck_ref,
    cv_ref,
    lists_ref,
    gain_hbm,
    bq_hbm,
    bk_hbm,
    bv_hbm,
    table_hbm,
    out_ref,
    wbuf,
    kvbuf,
    tokbuf,
    normed,
    cosine,
    sine,
    qbuf,
    knew,
    vnew,
    ostage,
    gain_ref,
    bias_ref,
    flat_gain,
    flat_bq,
    flat_bk,
    flat_bv,
    table_ref,
    lvmem,
    lsmem,
    load_sem,
    z_recv,
    z_recv_across,
    y_recv,
    z_send,
    y_send,
    x_recv,
    x_send,
    kv_load,
    kv_recv,
    kv_send,
    misc_sem,
    misc_send,
    out_send,
    out_recv,
):
    ctx = lax.axis_index("ctx")
    grp = lax.axis_index("grp")
    core = ctx % 2
    y_hi = (ctx // 2) % 2
    x = ctx // 4
    y_lo = grp // NZ
    z = grp % NZ
    y = y_hi * 2 + y_lo
    rows = tok_ref.shape[0]

    partner = device_of(x, y, z, 1 - core)
    xp = device_of((x + 1) % NX, y, z, core)
    xm = device_of((x + 3) % NX, y, z, core)
    yp = device_of(x, (y + 1) % NY, z, core)
    ym = device_of(x, (y + 3) % NY, z, core)
    zp = device_of(x, y, (z + 1) % NZ, core)
    zm = device_of(x, y, (z + 7) % NZ, core)
    ykv = device_of(x, (y + 3 + 2 * (y % 2)) % NY, z, core)
    yother = device_of(x, (y + 1 + 2 * (y % 2)) % NY, z, core)

    def remote(src, dst, send_sem, recv_sem, device):
        return pltpu.make_async_remote_copy(
            src_ref=src,
            dst_ref=dst,
            send_sem=send_sem,
            recv_sem=recv_sem,
            device_id=device,
            device_id_type=MESH,
        )

    def columns(index):
        return pl.ds(pl.multiple_of(index * HD, HD), HD)

    def slot_of(i):
        return 10 + x if i == 0 else PLACE[i]

    tok_load = pltpu.make_async_copy(tok_ref, tokbuf.at[0], misc_sem.at[0])
    loads = []
    for i in range(CHUNKS):
        place = PLACE[i]
        if i == 0:
            src = wq_ref.at[:, columns(core * 10 + x)]
        elif place < 4:
            ref = wk_ref if place % 2 == 0 else wv_ref
            src = ref.at[:, columns(core * 2 + place // 2)]
        else:
            src = wq_ref.at[:, columns(core * 10 + place)]
        loads.append(pltpu.make_async_copy(src, wbuf.at[slot_of(i), grp], load_sem.at[i]))
    kv_loads = []
    for part in range(4):
        ref = ck_ref if part < 2 else cv_ref
        kv_loads.append(
            pltpu.make_async_copy(
                ref.at[:, columns(core * 2 + part % 2)], kvbuf.at[ctx, part], kv_load.at[part]
            )
        )
    list_load = pltpu.make_async_copy(lists_ref, lsmem.at[0], misc_sem.at[3])
    table_load = pltpu.make_async_copy(table_hbm, table_ref, misc_sem.at[5])
    flat_loads = [
        pltpu.make_async_copy(src, dst, misc_sem.at[6 + n])
        for n, (src, dst) in enumerate(
            (
                (gain_hbm, flat_gain),
                (bq_hbm, flat_bq),
                (bk_hbm, flat_bk),
                (bv_hbm, flat_bv),
            )
        )
    ]
    for copy in kv_loads + loads[:AHEAD] + [tok_load] + flat_loads + [table_load, list_load] + loads[AHEAD:]:
        copy.start()

    barrier = pltpu.get_barrier_semaphore()
    for device in (partner, xp, xm, yp, ym, zp, zm):
        pl.semaphore_signal(barrier, inc=1, device_id=device, device_id_type=MESH)
    pl.semaphore_wait(barrier, 7)

    shard_rows = wbuf.shape[2]
    half = shard_rows // 2

    def send_y(i, slot, shard, distance):
        row = y_lo * NZ + shard
        cut = half - 16 if distance <= 1 else half
        lower, upper = wbuf.at[slot, row, 0:cut], wbuf.at[slot, row, cut:shard_rows]
        remote(lower, lower, y_send.at[i], y_recv.at[i], ykv).start()
        remote(upper, upper, y_send.at[i], y_recv.at[i], yother).start()

    def send_z(i, slot, distance, line, wait=False):
        base = (y_lo if line == 0 else 1 - y_lo) * NZ
        back = 0 if wait else 1
        rightward = wbuf.at[slot, base + (z + 8 - distance + back) % NZ]
        leftward = wbuf.at[slot, base + (z + distance - back) % NZ]
        if distance == 4:
            rightward, leftward = rightward.at[0:half], leftward.at[half:shard_rows]
        recv = [
            z_recv.at[i, n] if line == 0 else z_recv_across.at[n]
            for n in (distance - 1, 3 + distance)
        ]
        copies = (
            remote(rightward, rightward, z_send.at[i], recv[0], zp),
            remote(leftward, leftward, z_send.at[i], recv[1], zm),
        )
        for copy in copies:
            if wait:
                copy.wait_recv()
            else:
                copy.start()

    def send_own(i):
        slot = slot_of(i)
        loads[i].wait()
        send_z(i, slot, 1, 0)
        send_y(i, slot, z, 0)

    def pass_on(i, distance, line):
        slot = slot_of(i)
        send_z(i, slot, distance, line, wait=True)
        if distance < 4:
            send_z(i, slot, distance + 1, line)
        if i in Y_FIRST:
            return
        send_y(i, slot, (z + 8 - distance) % NZ, distance)
        if distance < 4:
            send_y(i, slot, (z + distance) % NZ, distance)

    def send_across(i):
        slot = slot_of(i)
        landed = wbuf.at[slot, (1 - y_lo) * NZ + z]
        remote(landed, landed, y_send.at[i], y_recv.at[i], ykv).wait_recv()
        send_z(i, slot, 1, 1)

    def wait_y(i):
        if i in Y_FIRST:
            return
        landed = wbuf.at[slot_of(i), pl.ds((1 - y_lo) * NZ, NZ)]
        remote(landed, landed, y_send.at[i], y_recv.at[i], ykv).wait_recv()

    kv_parts = []
    for part in range(4):
        ref = ck_ref if part < 2 else cv_ref
        kv_parts.append(
            remote(
                ref.at[:, columns((1 - core) * 2 + part % 2)],
                kvbuf.at[ctx, part],
                kv_send.at[0],
                kv_recv.at[0],
                partner,
            )
        )

    def pair(at_x, at_y):
        return kvbuf.at[pl.ds(at_x * 4 + at_y * 2, 2)]

    left_x, right_x, far_x = (x + 3) % NX, (x + 1) % NX, (x + 2) % NX
    kv_y = remote(pair(x, y_hi), pair(x, y_hi), kv_send.at[1], kv_recv.at[1], ykv)
    kv_x = [
        remote(pair(x, y_hi), pair(x, y_hi), kv_send.at[2], kv_recv.at[2], xp),
        remote(pair(x, y_hi), pair(x, y_hi), kv_send.at[3], kv_recv.at[3], xm),
        remote(pair(x, 1 - y_hi), pair(x, 1 - y_hi), kv_send.at[4], kv_recv.at[4], xp),
        remote(pair(x, 1 - y_hi), pair(x, 1 - y_hi), kv_send.at[5], kv_recv.at[5], xm),
        remote(pair(left_x, y_hi), pair(left_x, y_hi), kv_send.at[6], kv_recv.at[6], xp),
        remote(
            pair(right_x, 1 - y_hi), pair(right_x, 1 - y_hi), kv_send.at[7], kv_recv.at[7], xm
        ),
    ]

    def shared(at_x, upper):
        return wbuf.at[10 + at_x, 8:16] if upper else wbuf.at[10 + at_x, 0:8]

    x_copies = [
        remote(shared(x, 0), shared(x, 0), x_send.at[0], x_recv.at[0], xp),
        remote(shared(x, 1), shared(x, 1), x_send.at[1], x_recv.at[1], xm),
        remote(shared(x, 1), shared(x, 1), x_send.at[2], x_recv.at[2], xp),
        remote(shared(x, 0), shared(x, 0), x_send.at[3], x_recv.at[3], xm),
        remote(shared(left_x, 0), shared(left_x, 0), x_send.at[4], x_recv.at[4], xp),
        remote(shared(right_x, 1), shared(right_x, 1), x_send.at[5], x_recv.at[5], xm),
    ]

    def norm_rows(part):
        @pl.loop(0, rows // 64)
        def _(step):
            at = pl.ds(pl.multiple_of(step * 64, 64), 64)
            wide = tokbuf[part, at, :].astype(jnp.float32)
            mean = jnp.mean(wide * wide, axis=-1, keepdims=True)
            scaled = wide * lax.rsqrt(mean + norm_eps) * gain_ref[0:1, :]
            normed[pl.ds(pl.multiple_of(part * rows + step * 64, 64), 64), :] = scaled.astype(
                jnp.bfloat16
            )

    def tables():
        lane = lax.broadcasted_iota(jnp.int32, (QBLK, HD), 1)
        sign = jnp.where(lane < HD // 2, -1.0, 1.0)

        @pl.loop(0, 2 * rows // QBLK)
        def _(step):
            of_ctx = jnp.where(step < rows // QBLK, ctx, ctx + 1 - 2 * core)
            first = (of_ctx * 16 + grp) * rows + (step % (rows // QBLK)) * QBLK
            position = start_ref[0] + first + lax.broadcasted_iota(jnp.int32, (QBLK, HD), 0)
            angle = jnp.zeros((QBLK, HD), jnp.float32)
            for level in range(4):
                digit = ((position >> (5 * level)) & 31).astype(jnp.float32)
                angle = angle + digit * table_ref[level : level + 1, :]
            turns = jnp.floor(angle * (1.0 / (2.0 * math.pi)) + 0.5)
            angle = (angle - turns * 6.28125) - turns * (2.0 * math.pi - 6.28125)
            at = pl.ds(pl.multiple_of(step * QBLK, QBLK), QBLK)
            cosine[at, :] = jnp.cos(angle)
            sine[at, :] = jnp.sin(angle) * sign

    def project(slots, bias_rows):
        weights = [wbuf[slot].reshape(normed.shape[1], HD) for slot in slots]
        linear = jnp.dot(
            normed[...], jnp.concatenate(weights, axis=1), preferred_element_type=jnp.float32
        )
        return [
            linear[:, n * HD : (n + 1) * HD] + bias_ref[pl.ds(row, 1), :]
            for n, row in enumerate(bias_rows)
        ]

    def rope(linear):
        return linear * cosine[...] + pltpu.roll(linear, HD // 2, 1) * sine[...]

    def copy_out(slot, place):
        other, target = ostage.at[slot], out_ref.at[place]
        remote(other, target, out_send.at[0], out_recv.at[0], partner).start()

    def key_value_chunks(head):
        global_head = core * 2 + head
        linear_key, linear_value = project(
            (2 * head, 2 * head + 1), (20 + global_head, 24 + global_head)
        )
        key = rope(linear_key)
        knew[head] = key.astype(jnp.bfloat16)
        ostage[2 * head] = key[rows:]
        copy_out(2 * head, 20 + global_head)
        out_ref[20 + global_head] = key[:rows]
        vnew[head] = linear_value.astype(jnp.bfloat16)
        ostage[2 * head + 1] = linear_value[rows:]
        copy_out(2 * head + 1, 24 + global_head)
        out_ref[24 + global_head] = linear_value[:rows]

    scale = HD**-0.5 * math.log2(math.e)
    row_at = lax.broadcasted_iota(jnp.int32, (QBLK, QBLK), 0)
    column_at = lax.broadcasted_iota(jnp.int32, (QBLK, QBLK), 1)
    blocks = rows // QBLK

    def attend(n, slot):
        local = slot % 10
        head = local // GROUP
        scores, values = [], []
        for block in range(2 * blocks):
            at = slice(block * QBLK, (block + 1) * QBLK)
            keys, shifts = [], []
            values.append([])
            for step in range(SEL):
                index = lsmem[block // blocks, block % blocks, step, core * 10 + local]
                shifts.append(jnp.where(index >= 0, 0.0, -jnp.inf))
                index = jnp.maximum(index, 0)
                keys.append(kvbuf[index, head])
                values[-1].append(kvbuf[index, 2 + head])
            keys.append(knew[head, at, :])
            values[-1].append(vnew[head, at, :])
            all_keys = lax.dot_general(
                qbuf[n, at, :],
                jnp.concatenate(keys, axis=0),
                (((1,), (1,)), ((), ())),
                preferred_element_type=jnp.float32,
            )
            parts = [
                all_keys[:, step * QBLK : (step + 1) * QBLK] + shifts[step] for step in range(SEL)
            ]
            near = all_keys[:, SEL * QBLK :]
            scores.append(parts + [jnp.where(row_at >= column_at, near, -jnp.inf)])
        largest = [
            jnp.max(functools.reduce(jnp.maximum, parts), axis=1, keepdims=True)
            for parts in scores
        ]
        for block in list(range(blocks, 2 * blocks)) + list(range(blocks)):
            weights = [jnp.exp2(part - largest[block]) for part in scores[block]]
            total = jnp.sum(functools.reduce(jnp.add, weights), axis=1, keepdims=True)
            mixed = jnp.dot(
                jnp.concatenate([part.astype(jnp.bfloat16) for part in weights], axis=1),
                jnp.concatenate(values[block], axis=0),
                preferred_element_type=jnp.float32,
            )
            result = mixed * (1.0 / total)
            at = slice(block % blocks * QBLK, (block % blocks + 1) * QBLK)
            if block >= blocks:
                ostage[slot, at, :] = result
            else:
                out_ref[core * 10 + local, at, :] = result
            if block == 2 * blocks - 1:
                copy_out(slot, core * 10 + local)

    def query_chunks(first, second):
        heads = (core * 10 + first % 10, core * 10 + second % 10)
        linear = project((first, second), heads)
        for n in range(2):
            qbuf[n] = (rope(linear[n]) * scale).astype(jnp.bfloat16)

    tok_send = remote(tok_ref, tokbuf.at[1], misc_send.at[0], misc_sem.at[1], partner)
    list_send = remote(lists_ref, lvmem, misc_send.at[1], misc_sem.at[2], partner)

    def kv_wait(landed, number):
        remote(landed, landed, kv_send.at[number], kv_recv.at[number], xp).wait_recv()

    def shared_wait(landed, number):
        remote(landed, landed, x_send.at[number], x_recv.at[number], xp).wait_recv()

    def run(op):
        kind, at = op[0], op[1:]
        if kind == "own":
            send_own(*at)
        elif kind == "z":
            pass_on(*at)
        elif kind == "yf":
            send_across(*at)
        elif kind == "y":
            wait_y(*at)
        elif kind == "kv0":
            for copy in kv_loads:
                copy.wait()
            kv_wait(kvbuf.at[ctx + 1 - 2 * core], 0)
            kv_y.start()
            kv_x[0].start()
            kv_x[1].start()
        elif kind == "kv1":
            kv_wait(pair(x, 1 - y_hi), 1)
            kv_x[2].start()
            kv_x[3].start()
        elif kind == "kv2":
            kv_wait(pair(left_x, y_hi), 2)
            kv_x[4].start()
        elif kind == "kv3":
            kv_wait(pair(right_x, 1 - y_hi), 5)
            kv_x[5].start()
        elif kind == "kvw":
            kv_wait(pair(right_x, y_hi), 3)
            kv_wait(pair(left_x, 1 - y_hi), 4)
            kv_wait(pair(far_x, y_hi), 6)
            kv_wait(pair(far_x, 1 - y_hi), 7)
        elif kind == "b0":
            wait_y(0)
            for copy in x_copies[:4]:
                copy.start()
        elif kind == "b1":
            shared_wait(shared(left_x, 0), 0)
            shared_wait(shared(right_x, 1), 1)
            x_copies[4].start()
            x_copies[5].start()
        elif kind == "b2":
            shared_wait(shared(left_x, 1), 2)
            shared_wait(shared(right_x, 0), 3)
        elif kind == "b3":
            shared_wait(shared(far_x, 0), 4)
            shared_wait(shared(far_x, 1), 5)

    for copy in kv_parts:
        copy.start()
    for op in SCHEDULE[0][0][:AHEAD]:
        run(op)
    list_send.start()
    tok_send.start()
    table_load.wait()
    for copy in flat_loads:
        copy.wait()
    gain_ref[0:1, :] = flat_gain[...].astype(jnp.float32).reshape(1, gain_ref.shape[1])
    row = 0
    for flat in (flat_bq, flat_bk, flat_bv):
        for step in range(flat.shape[0] // HD):
            piece = flat[step * HD : (step + 1) * HD].astype(jnp.float32)
            bias_ref[row : row + 1, :] = piece.reshape(1, HD)
            row += 1

    pairs = (
        (10 + x, 4),
        (5, 6),
        (7, 8),
        (10 + left_x, 10 + right_x),
        (9, 10 + far_x),
    )
    units = [unit for _, unit in SCHEDULE]

    @pl.loop(0, len(SCHEDULE))
    def _(now):
        for number, (ops, _unused) in enumerate(SCHEDULE):
            rest = ops[AHEAD:] if number == 0 else ops
            if rest:

                @pl.when(now == number)
                def _():
                    for op in rest:
                        run(op)

        def on(kind):
            places = [n for n, unit in enumerate(units) if unit[0] == kind]
            condition = functools.reduce(jnp.logical_or, [now == n for n in places])

            def pick(values):
                value = values[units[places[-1]][1]]
                for n in places[:-1]:
                    value = jnp.where(now == n, values[units[n][1]], value)
                return value

            return condition, pick

        @pl.when(on("N0")[0])
        def _():
            tok_load.wait()
            norm_rows(0)

        @pl.when(on("T")[0])
        def _():
            tables()

        @pl.when(on("N1")[0])
        def _():
            tok_send.wait_recv()
            norm_rows(1)
            list_send.wait_recv()
            list_load.wait()
            move = pltpu.make_async_copy(lvmem, lsmem.at[1], misc_sem.at[4])
            move.start()
            move.wait()

        condition, pick_pair = on("K")

        @pl.when(condition)
        def _():
            key_value_chunks(pick_pair((0, 1)))

        condition, pick_query = on("P")

        @pl.when(condition)
        def _():
            query_chunks(
                pick_query([first for first, _ in pairs]),
                pick_query([second for _, second in pairs]),
            )

        condition, pick_head = on("A")

        @pl.when(condition)
        def _():
            flat = [slot for both in pairs for slot in both]
            attend(pick_head([n % 2 for n in range(len(flat))]), pick_head(flat))

    for i in range(CHUNKS):
        sent = wbuf.at[0, 0:14] if i in Y_FIRST else wbuf.at[0, 0:7]
        pltpu.make_async_copy(sent, sent, z_send.at[i]).wait()
        sent = wbuf.at[0, 0] if i in Y_FIRST else wbuf.at[0, 0:8]
        pltpu.make_async_copy(sent, sent, y_send.at[i]).wait()

    for copy in x_copies:
        copy.wait_send()
    pltpu.make_async_copy(kvbuf.at[0], kvbuf.at[0], kv_send.at[0]).wait()
    kv_y.wait_send()
    for copy in kv_x:
        copy.wait_send()
    tok_send.wait_send()
    list_send.wait_send()
    written = ostage
    pltpu.make_async_copy(written, written, out_send.at[0]).wait()
    pltpu.make_async_copy(written, written, out_recv.at[0]).wait()


def write_kernel(source, ctx_ref, keys_ref, values_ref, sem):
    copies = []
    for place in range(28):
        target, first = ((ctx_ref, 0), (keys_ref, 20), (values_ref, 24))[
            (place >= 20) + (place >= 24)
        ]
        column = (place - first) * HD
        copies.append(
            pltpu.make_async_copy(
                source.at[place], target.at[:, column : column + HD], sem.at[place]
            )
        )
    for copy in copies:
        copy.start()
    for copy in copies:
        copy.wait()


def on_device(
    tokens,
    norm_gain,
    w_query,
    w_key,
    w_value,
    b_query,
    b_key,
    b_value,
    cache_keys,
    cache_values,
    block_lists,
    start_position,
):
    rows, features = tokens.shape
    shard = w_query.shape[0]
    lists = jnp.transpose(block_lists, (1, 2, 0))
    table = jnp.asarray(np.pad(angle_tables(HD), ((0, 4), (0, 0))), jnp.float32)
    hbm = pl.BlockSpec(memory_space=pltpu.HBM)
    vmem = pl.BlockSpec(memory_space=pltpu.VMEM)
    smem = pl.BlockSpec(memory_space=pltpu.SMEM)
    dma = pltpu.SemaphoreType.DMA
    heads_out = pl.pallas_call(
        kernel,
        out_shape=pltpu.VMEM((28, rows, HD), jnp.float32),
        in_specs=[smem] + [hbm] * 12,
        out_specs=pl.BlockSpec(memory_space=pltpu.VMEM),
        scratch_shapes=[
            pltpu.VMEM((14, 16, shard, HD), jnp.bfloat16),
            pltpu.VMEM((16, 4, QBLK, HD), jnp.bfloat16),
            pltpu.VMEM((2, rows, features), jnp.bfloat16),
            pltpu.VMEM((2 * rows, features), jnp.bfloat16),
            pltpu.VMEM((2 * rows, HD), jnp.float32),
            pltpu.VMEM((2 * rows, HD), jnp.float32),
            pltpu.VMEM((2, 2 * rows, HD), jnp.bfloat16),
            pltpu.VMEM((2, 2 * rows, HD), jnp.bfloat16),
            pltpu.VMEM((2, 2 * rows, HD), jnp.bfloat16),
            pltpu.VMEM((14, rows, HD), jnp.float32),
            pltpu.VMEM((8, features), jnp.float32),
            pltpu.VMEM((32, HD), jnp.float32),
            pltpu.VMEM(norm_gain.shape, jnp.bfloat16),
            pltpu.VMEM(b_query.shape, jnp.bfloat16),
            pltpu.VMEM(b_key.shape, jnp.bfloat16),
            pltpu.VMEM(b_value.shape, jnp.bfloat16),
            pltpu.VMEM((8, HD), jnp.float32),
            pltpu.VMEM(lists.shape, jnp.int32),
            pltpu.SMEM((2,) + lists.shape, jnp.int32),
            dma((CHUNKS,)),
            dma((CHUNKS, 8)),
            dma((8,)),
            dma((CHUNKS,)),
            dma((CHUNKS,)),
            dma((CHUNKS,)),
            dma((6,)),
            dma((6,)),
            dma((4,)),
            dma((8,)),
            dma((8,)),
            dma((10,)),
            dma((2,)),
            dma((1,)),
            dma((1,)),
        ],
        compiler_params=pltpu.CompilerParams(
            collective_id=0, has_side_effects=True, vmem_limit_bytes=58 << 20
        ),
        name="gather_attend",
    )(
        start_position,
        tokens,
        w_query,
        w_key,
        w_value,
        cache_keys,
        cache_values,
        lists,
        norm_gain,
        b_query,
        b_key,
        b_value,
        table,
    )
    return pl.pallas_call(
        write_kernel,
        out_shape=(
            jax.ShapeDtypeStruct((rows, 20 * HD), jnp.float32),
            jax.ShapeDtypeStruct((rows, 4 * HD), jnp.float32),
            jax.ShapeDtypeStruct((rows, 4 * HD), jnp.float32),
        ),
        in_specs=[vmem],
        out_specs=[hbm] * 3,
        scratch_shapes=[dma((28,))],
        compiler_params=pltpu.CompilerParams(vmem_limit_bytes=4 << 20),
        name="write_out",
    )(heads_out)


def solution(mesh):
    in_specs = (
        P(("ctx", "grp"), None),
        P(),
        P("grp", None),
        P("grp", None),
        P("grp", None),
        P(),
        P(),
        P(),
        P("ctx", None),
        P("ctx", None),
        P(None, ("ctx", "grp"), None),
        P(),
    )
    out_specs = (P(("ctx", "grp"), None), P(("ctx", "grp"), None), P(("ctx", "grp"), None))
    return jax.shard_map(
        on_device, mesh=mesh, in_specs=in_specs, out_specs=out_specs, check_vma=False
    )
```

```python
import functools
import math

import jax
import jax.numpy as jnp
import numpy as np
from jax import lax
from jax.experimental import pallas as pl
from jax.experimental.pallas import tpu as pltpu
from jax.sharding import PartitionSpec as P

MESH = pl.DeviceIdType.MESH

HD = 128
GROUP = 5
QBLK = 128
SEL = 4

norm_eps = 1e-06
rope_base = 10000000.0

NX, NY, NZ = 4, 4, 8
CHUNKS = 11
PLACE = (None, 0, 1, 4, 2, 3, 5, 6, 7, 8, 9)

Y_FIRST = (8,)
NEAR = 1
SCHEDULE = (
    ((
        ("own", 0), ("own", 3), ("kv0", 0), ("own", 1), ("own", 5), ("own", 2), ("kv0", 1),
        ("z", 0, 1, 0), ("z", 3, 1, 0),
    ), ("N0",)),
    ((
        ("own", 4), ("z", 5, 1, 0), ("z", 1, 1, 0), ("kv1", 0),
    ), ("T",)),
    ((
        ("z", 0, 2, 0), ("z", 2, 1, 0), ("z", 3, 2, 0), ("kv2", 0), ("z", 4, 1, 0), ("kv1", 1),
        ("z", 1, 2, 0), ("z", 0, 3, 0), ("own", 7), ("own", 6), ("z", 2, 2, 0), ("own", 8),
        ("kv3", 0), ("kv2", 1), ("z", 0, 4, 0), ("z", 4, 2, 0), ("z", 3, 3, 0), ("kv3", 1),
        ("z", 5, 2, 0), ("z", 1, 3, 0), ("z", 2, 3, 0), ("z", 7, 1, 0), ("b0",), ("own", 9),
    ), ("N1",)),
    ((
        ("yf", 8), ("own", 10), ("z", 3, 4, 0), ("z", 2, 4, 0), ("z", 4, 3, 0), ("z", 1, 4, 0),
        ("z", 5, 3, 0), ("z", 6, 1, 0), ("z", 9, 1, 0), ("z", 7, 2, 0), ("z", 10, 1, 0),
        ("z", 8, 1, 0), ("kvw",), ("z", 5, 4, 0), ("z", 4, 4, 0), ("y", 2), ("z", 6, 2, 0),
        ("y", 1), ("y", 3), ("z", 8, 1, 1),
    ), ("K", 0)),
    ((
        ("z", 7, 3, 0), ("z", 9, 2, 0), ("z", 10, 2, 0),
    ), ("P", 0)),
    ((
        ("z", 6, 3, 0), ("b1",), ("z", 8, 2, 0),
    ), ("A", 0)),
    ((
        ("z", 8, 2, 1), ("y", 4), ("z", 7, 4, 0), ("y", 5), ("z", 9, 3, 0),
    ), ("K", 1)),
    ((
        ("z", 6, 4, 0), ("z", 10, 3, 0), ("z", 8, 3, 0), ("b2",),
    ), ("P", 3)),
    ((
        ("z", 8, 3, 1), ("z", 9, 4, 0),
    ), ("A", 3)),
    ((
        ("z", 10, 4, 0), ("y", 7), ("y", 6),
    ), ("P", 1)),
    ((

    ), ("A", 1)),
    ((
        ("y", 9), ("z", 8, 4, 1), ("z", 8, 4, 0), ("y", 8),
    ), ("P", 2)),
    ((

    ), ("A", 2)),
    ((
        ("y", 10), ("b3",),
    ), ("P", 4)),
    ((

    ), ("A", 4)),
)
AHEAD = [op[0] == "own" for op in SCHEDULE[0][0] + (("",),)].index(False)


def angle_tables(head_dim):
    half_dim = head_dim // 2
    frequency = rope_base ** (-2.0 * np.arange(half_dim) / head_dim)
    tables = np.stack(
        [np.mod(frequency * 32.0**digit_level, 2.0 * np.pi) for digit_level in range(4)]
    )
    return np.concatenate([tables, tables], axis=1)


def device_of(x, y, z, core):
    return (x * 4 + (y // 2) * 2 + core, (y % 2) * NZ + z)


def kernel(
    start_ref,
    tok_ref,
    wq_ref,
    wk_ref,
    wv_ref,
    ck_ref,
    cv_ref,
    lists_ref,
    gain_hbm,
    bq_hbm,
    bk_hbm,
    bv_hbm,
    table_hbm,
    out_ref,
    wbuf,
    kvbuf,
    tokbuf,
    normed,
    cosine,
    sine,
    qbuf,
    knew,
    vnew,
    ostage,
    gain_ref,
    bias_ref,
    flat_gain,
    flat_bq,
    flat_bk,
    flat_bv,
    table_ref,
    lvmem,
    lsmem,
    load_sem,
    z_recv,
    z_recv_across,
    y_recv,
    z_send,
    y_send,
    x_recv,
    x_send,
    kv_load,
    kv_recv,
    kv_send,
    misc_sem,
    misc_send,
    out_send,
    out_recv,
):
    ctx = lax.axis_index("ctx")
    grp = lax.axis_index("grp")
    core = ctx % 2
    y_hi = (ctx // 2) % 2
    x = ctx // 4
    y_lo = grp // NZ
    z = grp % NZ
    y = y_hi * 2 + y_lo
    rows = tok_ref.shape[0]

    partner = device_of(x, y, z, 1 - core)
    xp = device_of((x + 1) % NX, y, z, core)
    xm = device_of((x + 3) % NX, y, z, core)
    yp = device_of(x, (y + 1) % NY, z, core)
    ym = device_of(x, (y + 3) % NY, z, core)
    zp = device_of(x, y, (z + 1) % NZ, core)
    zm = device_of(x, y, (z + 7) % NZ, core)
    ykv = device_of(x, (y + 3 + 2 * (y % 2)) % NY, z, core)
    yother = device_of(x, (y + 1 + 2 * (y % 2)) % NY, z, core)

    def remote(src, dst, send_sem, recv_sem, device):
        return pltpu.make_async_remote_copy(
            src_ref=src,
            dst_ref=dst,
            send_sem=send_sem,
            recv_sem=recv_sem,
            device_id=device,
            device_id_type=MESH,
        )

    def columns(index):
        return pl.ds(pl.multiple_of(index * HD, HD), HD)

    def slot_of(i):
        return 10 + x if i == 0 else PLACE[i]

    barrier = pltpu.get_barrier_semaphore()
    for device in (partner, xp, xm, yp, ym, zp, zm):
        pl.semaphore_signal(barrier, inc=1, device_id=device, device_id_type=MESH)

    tok_load = pltpu.make_async_copy(tok_ref, tokbuf.at[0], misc_sem.at[0])
    loads = []
    for i in range(CHUNKS):
        place = PLACE[i]
        if i == 0:
            src = wq_ref.at[:, columns(core * 10 + x)]
        elif place < 4:
            ref = wk_ref if place % 2 == 0 else wv_ref
            src = ref.at[:, columns(core * 2 + place // 2)]
        else:
            src = wq_ref.at[:, columns(core * 10 + place)]
        loads.append(pltpu.make_async_copy(src, wbuf.at[slot_of(i), grp], load_sem.at[i]))
    kv_loads = []
    for part in range(4):
        ref = ck_ref if part < 2 else cv_ref
        kv_loads.append(
            pltpu.make_async_copy(
                ref.at[:, columns(core * 2 + part % 2)], kvbuf.at[ctx, part], kv_load.at[part]
            )
        )
    list_load = pltpu.make_async_copy(lists_ref, lsmem.at[0], misc_sem.at[3])
    table_load = pltpu.make_async_copy(table_hbm, table_ref, misc_sem.at[5])
    flat_loads = [
        pltpu.make_async_copy(src, dst, misc_sem.at[6 + n])
        for n, (src, dst) in enumerate(
            (
                (gain_hbm, flat_gain),
                (bq_hbm, flat_bq),
                (bk_hbm, flat_bk),
                (bv_hbm, flat_bv),
            )
        )
    ]
    for copy in kv_loads + loads[:AHEAD] + [tok_load] + flat_loads + [table_load, list_load] + loads[AHEAD:]:
        copy.start()

    pl.semaphore_wait(barrier, 7)

    shard_rows = wbuf.shape[2]
    half = shard_rows // 2

    def send_y(i, slot, shard, distance):
        row = y_lo * NZ + shard
        cut = half - 16 if distance <= NEAR else half
        lower, upper = wbuf.at[slot, row, 0:cut], wbuf.at[slot, row, cut:shard_rows]
        remote(lower, lower, y_send.at[i], y_recv.at[i], ykv).start()
        remote(upper, upper, y_send.at[i], y_recv.at[i], yother).start()

    def send_z(i, slot, distance, line, wait=False):
        base = (y_lo if line == 0 else 1 - y_lo) * NZ
        back = 0 if wait else 1
        rightward = wbuf.at[slot, base + (z + 8 - distance + back) % NZ]
        leftward = wbuf.at[slot, base + (z + distance - back) % NZ]
        if distance == 4:
            rightward, leftward = rightward.at[0:half], leftward.at[half:shard_rows]
        recv = [
            z_recv.at[i, n] if line == 0 else z_recv_across.at[n]
            for n in (distance - 1, 3 + distance)
        ]
        copies = (
            remote(rightward, rightward, z_send.at[i], recv[0], zp),
            remote(leftward, leftward, z_send.at[i], recv[1], zm),
        )
        for copy in copies:
            if wait:
                copy.wait_recv()
            else:
                copy.start()

    def send_own(i):
        slot = slot_of(i)
        loads[i].wait()
        send_z(i, slot, 1, 0)
        send_y(i, slot, z, 0)

    def pass_on(i, distance, line):
        slot = slot_of(i)
        send_z(i, slot, distance, line, wait=True)
        if distance < 4:
            send_z(i, slot, distance + 1, line)
        if i in Y_FIRST:
            return
        send_y(i, slot, (z + 8 - distance) % NZ, distance)
        if distance < 4:
            send_y(i, slot, (z + distance) % NZ, distance)

    def send_across(i):
        slot = slot_of(i)
        landed = wbuf.at[slot, (1 - y_lo) * NZ + z]
        remote(landed, landed, y_send.at[i], y_recv.at[i], ykv).wait_recv()
        send_z(i, slot, 1, 1)

    def wait_y(i):
        if i in Y_FIRST:
            return
        landed = wbuf.at[slot_of(i), pl.ds((1 - y_lo) * NZ, NZ)]
        remote(landed, landed, y_send.at[i], y_recv.at[i], ykv).wait_recv()

    kv_parts = []
    for part in range(4):
        ref = ck_ref if part < 2 else cv_ref
        kv_parts.append(
            remote(
                ref.at[:, columns((1 - core) * 2 + part % 2)],
                kvbuf.at[ctx, part],
                kv_send.at[0],
                kv_recv.at[0],
                partner,
            )
        )

    def cached(at_x, at_y, side):
        return kvbuf.at[at_x * 4 + at_y * 2 + (core if side == 0 else 1 - core)]

    left_x, right_x, far_x = (x + 3) % NX, (x + 1) % NX, (x + 2) % NX

    def kv_copy(number, side):
        at_x, at_y, device = (
            (x, y_hi, ykv),
            (x, y_hi, xp),
            (x, y_hi, xm),
            (x, 1 - y_hi, xp),
            (x, 1 - y_hi, xm),
            (left_x, y_hi, xp),
            (right_x, 1 - y_hi, xm),
        )[number]
        block = cached(at_x, at_y, side)
        number = 1 + 7 * side + number
        return remote(block, block, kv_send.at[number], kv_recv.at[number], device)

    def shared(at_x, upper):
        return wbuf.at[10 + at_x, 8:16] if upper else wbuf.at[10 + at_x, 0:8]

    x_copies = [
        remote(shared(x, 0), shared(x, 0), x_send.at[0], x_recv.at[0], xp),
        remote(shared(x, 1), shared(x, 1), x_send.at[1], x_recv.at[1], xm),
        remote(shared(x, 1), shared(x, 1), x_send.at[2], x_recv.at[2], xp),
        remote(shared(x, 0), shared(x, 0), x_send.at[3], x_recv.at[3], xm),
        remote(shared(left_x, 0), shared(left_x, 0), x_send.at[4], x_recv.at[4], xp),
        remote(shared(right_x, 1), shared(right_x, 1), x_send.at[5], x_recv.at[5], xm),
    ]

    def norm_rows(part):
        @pl.loop(0, rows // 64)
        def _(step):
            at = pl.ds(pl.multiple_of(step * 64, 64), 64)
            wide = tokbuf[part, at, :].astype(jnp.float32)
            mean = jnp.mean(wide * wide, axis=-1, keepdims=True)
            scaled = wide * lax.rsqrt(mean + norm_eps) * gain_ref[0:1, :]
            normed[pl.ds(pl.multiple_of(part * rows + step * 64, 64), 64), :] = scaled.astype(
                jnp.bfloat16
            )

    def tables():
        lane = lax.broadcasted_iota(jnp.int32, (QBLK, HD), 1)
        sign = jnp.where(lane < HD // 2, -1.0, 1.0)

        @pl.loop(0, 2 * rows // QBLK)
        def _(step):
            of_ctx = jnp.where(step < rows // QBLK, ctx, ctx + 1 - 2 * core)
            first = (of_ctx * 16 + grp) * rows + (step % (rows // QBLK)) * QBLK
            position = start_ref[0] + first + lax.broadcasted_iota(jnp.int32, (QBLK, HD), 0)
            angle = jnp.zeros((QBLK, HD), jnp.float32)
            for level in range(4):
                digit = ((position >> (5 * level)) & 31).astype(jnp.float32)
                angle = angle + digit * table_ref[level : level + 1, :]
            turns = jnp.floor(angle * (1.0 / (2.0 * math.pi)) + 0.5)
            angle = (angle - turns * 6.28125) - turns * (2.0 * math.pi - 6.28125)
            at = pl.ds(pl.multiple_of(step * QBLK, QBLK), QBLK)
            cosine[at, :] = jnp.cos(angle)
            sine[at, :] = jnp.sin(angle) * sign

    def project(slots, bias_rows):
        weights = [wbuf[slot].reshape(normed.shape[1], HD) for slot in slots]
        linear = jnp.dot(
            normed[...], jnp.concatenate(weights, axis=1), preferred_element_type=jnp.float32
        )
        return [
            linear[:, n * HD : (n + 1) * HD] + bias_ref[pl.ds(row, 1), :]
            for n, row in enumerate(bias_rows)
        ]

    def rope(linear):
        return linear * cosine[...] + pltpu.roll(linear, HD // 2, 1) * sine[...]

    def copy_out(slot, place):
        other, target = ostage.at[slot], out_ref.at[place]
        remote(other, target, out_send.at[0], out_recv.at[0], partner).start()

    def key_value_chunks(head):
        global_head = core * 2 + head
        linear_key, linear_value = project(
            (2 * head, 2 * head + 1), (20 + global_head, 24 + global_head)
        )
        key = rope(linear_key)
        knew[head] = key.astype(jnp.bfloat16)
        ostage[2 * head] = key[rows:]
        copy_out(2 * head, 20 + global_head)
        out_ref[20 + global_head] = key[:rows]
        vnew[head] = linear_value.astype(jnp.bfloat16)
        ostage[2 * head + 1] = linear_value[rows:]
        copy_out(2 * head + 1, 24 + global_head)
        out_ref[24 + global_head] = linear_value[:rows]

    scale = HD**-0.5 * math.log2(math.e)
    row_at = lax.broadcasted_iota(jnp.int32, (QBLK, QBLK), 0)
    column_at = lax.broadcasted_iota(jnp.int32, (QBLK, QBLK), 1)
    blocks = rows // QBLK

    def attend(slots):
        todo = [(n, block) for n in range(2) for block in range(2 * blocks)]
        scores, values = {}, {}
        for n, block in todo:
            local = slots[n] % 10
            head = local // GROUP
            at = slice(block * QBLK, (block + 1) * QBLK)
            keys, shifts = [], []
            values[n, block] = []
            for step in range(SEL):
                index = lsmem[block // blocks, block % blocks, step, core * 10 + local]
                shifts.append(jnp.where(index >= 0, 0.0, -jnp.inf))
                index = jnp.maximum(index, 0)
                keys.append(kvbuf[index, head])
                values[n, block].append(kvbuf[index, 2 + head])
            keys.append(knew[head, at, :])
            values[n, block].append(vnew[head, at, :])
            all_keys = lax.dot_general(
                qbuf[n, at, :],
                jnp.concatenate(keys, axis=0),
                (((1,), (1,)), ((), ())),
                preferred_element_type=jnp.float32,
            )
            parts = [
                all_keys[:, step * QBLK : (step + 1) * QBLK] + shifts[step] for step in range(SEL)
            ]
            near = all_keys[:, SEL * QBLK :]
            scores[n, block] = parts + [jnp.where(row_at >= column_at, near, -jnp.inf)]
        largest = {
            at: jnp.max(functools.reduce(jnp.maximum, scores[at]), axis=1, keepdims=True)
            for at in todo
        }
        for n, block in sorted(todo, key=lambda at: (at[1] < blocks, at)):
            weights = [jnp.exp2(part - largest[n, block]) for part in scores[n, block]]
            total = jnp.sum(functools.reduce(jnp.add, weights), axis=1, keepdims=True)
            mixed = jnp.dot(
                jnp.concatenate([part.astype(jnp.bfloat16) for part in weights], axis=1),
                jnp.concatenate(values[n, block], axis=0),
                preferred_element_type=jnp.float32,
            )
            result = mixed * (1.0 / total)
            place = core * 10 + slots[n] % 10
            at = slice(block % blocks * QBLK, (block % blocks + 1) * QBLK)
            if block >= blocks:
                ostage[slots[n], at, :] = result
            else:
                out_ref[place, at, :] = result
            if block == 2 * blocks - 1:
                copy_out(slots[n], place)

    def query_chunks(first, second):
        heads = (core * 10 + first % 10, core * 10 + second % 10)
        linear = project((first, second), heads)
        for n in range(2):
            qbuf[n] = (rope(linear[n]) * scale).astype(jnp.bfloat16)

    tok_send = remote(tok_ref, tokbuf.at[1], misc_send.at[0], misc_sem.at[1], partner)
    list_send = remote(lists_ref, lvmem, misc_send.at[1], misc_sem.at[2], partner)

    def kv_wait(landed, number, side):
        number = 1 + 7 * side + number
        remote(landed, landed, kv_send.at[number], kv_recv.at[number], xp).wait_recv()

    def shared_wait(landed, number):
        remote(landed, landed, x_send.at[number], x_recv.at[number], xp).wait_recv()

    def run(op):
        kind, at = op[0], op[1:]
        if kind == "own":
            send_own(*at)
        elif kind == "z":
            pass_on(*at)
        elif kind == "yf":
            send_across(*at)
        elif kind == "y":
            wait_y(*at)
        elif kind == "kv0":
            if at[0] == 0:
                for copy in kv_loads:
                    copy.wait()
            else:
                other = kvbuf.at[ctx + 1 - 2 * core]
                remote(other, other, kv_send.at[0], kv_recv.at[0], partner).wait_recv()
            for number in range(3):
                kv_copy(number, at[0]).start()
        elif kind == "kv1":
            kv_wait(cached(x, 1 - y_hi, at[0]), 0, at[0])
            kv_copy(3, at[0]).start()
            kv_copy(4, at[0]).start()
        elif kind == "kv2":
            kv_wait(cached(left_x, y_hi, at[0]), 1, at[0])
            kv_copy(5, at[0]).start()
        elif kind == "kv3":
            kv_wait(cached(right_x, 1 - y_hi, at[0]), 4, at[0])
            kv_copy(6, at[0]).start()
        elif kind == "kvw":
            for side in range(2):
                kv_wait(cached(right_x, y_hi, side), 2, side)
                kv_wait(cached(left_x, 1 - y_hi, side), 3, side)
                kv_wait(cached(far_x, y_hi, side), 5, side)
                kv_wait(cached(far_x, 1 - y_hi, side), 6, side)
        elif kind == "b0":
            wait_y(0)
            for copy in x_copies[:4]:
                copy.start()
        elif kind == "b1":
            shared_wait(shared(left_x, 0), 0)
            shared_wait(shared(right_x, 1), 1)
            x_copies[4].start()
            x_copies[5].start()
        elif kind == "b2":
            shared_wait(shared(left_x, 1), 2)
            shared_wait(shared(right_x, 0), 3)
        elif kind == "b3":
            shared_wait(shared(far_x, 0), 4)
            shared_wait(shared(far_x, 1), 5)

    for copy in kv_parts:
        copy.start()
    for op in SCHEDULE[0][0][:AHEAD]:
        run(op)
    list_send.start()
    tok_send.start()
    table_load.wait()
    for copy in flat_loads:
        copy.wait()
    gain_ref[0:1, :] = flat_gain[...].astype(jnp.float32).reshape(1, gain_ref.shape[1])
    row = 0
    for flat in (flat_bq, flat_bk, flat_bv):
        for step in range(flat.shape[0] // HD):
            piece = flat[step * HD : (step + 1) * HD].astype(jnp.float32)
            bias_ref[row : row + 1, :] = piece.reshape(1, HD)
            row += 1

    pairs = (
        (10 + x, 4),
        (5, 6),
        (7, 8),
        (10 + left_x, 10 + right_x),
        (9, 10 + far_x),
    )
    units = [unit for _, unit in SCHEDULE]

    @pl.loop(0, len(SCHEDULE))
    def _(now):
        for number, (ops, _unused) in enumerate(SCHEDULE):
            rest = ops[AHEAD:] if number == 0 else ops
            if rest:

                @pl.when(now == number)
                def _():
                    for op in rest:
                        run(op)

        def on(kind):
            places = [n for n, unit in enumerate(units) if unit[0] == kind]
            condition = functools.reduce(jnp.logical_or, [now == n for n in places])

            def pick(values):
                value = values[units[places[-1]][1]]
                for n in places[:-1]:
                    value = jnp.where(now == n, values[units[n][1]], value)
                return value

            return condition, pick

        @pl.when(on("N0")[0])
        def _():
            tok_load.wait()
            norm_rows(0)

        @pl.when(on("T")[0])
        def _():
            tables()

        @pl.when(on("N1")[0])
        def _():
            tok_send.wait_recv()
            norm_rows(1)
            list_send.wait_recv()
            list_load.wait()
            move = pltpu.make_async_copy(lvmem, lsmem.at[1], misc_sem.at[4])
            move.start()
            move.wait()

        condition, pick_pair = on("K")

        @pl.when(condition)
        def _():
            key_value_chunks(pick_pair((0, 1)))

        condition, pick_query = on("P")

        @pl.when(condition)
        def _():
            query_chunks(
                pick_query([first for first, _ in pairs]),
                pick_query([second for _, second in pairs]),
            )

        condition, pick_heads = on("A")

        @pl.when(condition)
        def _():
            attend(
                (
                    pick_heads([first for first, _ in pairs]),
                    pick_heads([second for _, second in pairs]),
                )
            )

    for i in range(CHUNKS):
        sent = wbuf.at[0, 0:14] if i in Y_FIRST else wbuf.at[0, 0:7]
        pltpu.make_async_copy(sent, sent, z_send.at[i]).wait()
        sent = wbuf.at[0, 0] if i in Y_FIRST else wbuf.at[0, 0:8]
        pltpu.make_async_copy(sent, sent, y_send.at[i]).wait()

    for copy in x_copies:
        copy.wait_send()
    pltpu.make_async_copy(kvbuf.at[0], kvbuf.at[0], kv_send.at[0]).wait()
    for side in range(2):
        for number in range(7):
            kv_copy(number, side).wait_send()
    tok_send.wait_send()
    list_send.wait_send()
    written = ostage
    pltpu.make_async_copy(written, written, out_send.at[0]).wait()
    pltpu.make_async_copy(written, written, out_recv.at[0]).wait()


def write_kernel(source, ctx_ref, keys_ref, values_ref, sem):
    copies = []
    for place in range(28):
        target, first = ((ctx_ref, 0), (keys_ref, 20), (values_ref, 24))[
            (place >= 20) + (place >= 24)
        ]
        column = (place - first) * HD
        copies.append(
            pltpu.make_async_copy(
                source.at[place], target.at[:, column : column + HD], sem.at[place]
            )
        )
    for copy in copies:
        copy.start()
    for copy in copies:
        copy.wait()


def on_device(
    tokens,
    norm_gain,
    w_query,
    w_key,
    w_value,
    b_query,
    b_key,
    b_value,
    cache_keys,
    cache_values,
    block_lists,
    start_position,
):
    rows, features = tokens.shape
    shard = w_query.shape[0]
    lists = jnp.transpose(block_lists, (1, 2, 0))
    table = jnp.asarray(np.pad(angle_tables(HD), ((0, 4), (0, 0))), jnp.float32)
    hbm = pl.BlockSpec(memory_space=pltpu.HBM)
    vmem = pl.BlockSpec(memory_space=pltpu.VMEM)
    smem = pl.BlockSpec(memory_space=pltpu.SMEM)
    dma = pltpu.SemaphoreType.DMA
    heads_out = pl.pallas_call(
        kernel,
        out_shape=pltpu.VMEM((28, rows, HD), jnp.float32),
        in_specs=[smem] + [hbm] * 12,
        out_specs=pl.BlockSpec(memory_space=pltpu.VMEM),
        scratch_shapes=[
            pltpu.VMEM((14, 16, shard, HD), jnp.bfloat16),
            pltpu.VMEM((16, 4, QBLK, HD), jnp.bfloat16),
            pltpu.VMEM((2, rows, features), jnp.bfloat16),
            pltpu.VMEM((2 * rows, features), jnp.bfloat16),
            pltpu.VMEM((2 * rows, HD), jnp.float32),
            pltpu.VMEM((2 * rows, HD), jnp.float32),
            pltpu.VMEM((2, 2 * rows, HD), jnp.bfloat16),
            pltpu.VMEM((2, 2 * rows, HD), jnp.bfloat16),
            pltpu.VMEM((2, 2 * rows, HD), jnp.bfloat16),
            pltpu.VMEM((14, rows, HD), jnp.float32),
            pltpu.VMEM((8, features), jnp.float32),
            pltpu.VMEM((32, HD), jnp.float32),
            pltpu.VMEM(norm_gain.shape, jnp.bfloat16),
            pltpu.VMEM(b_query.shape, jnp.bfloat16),
            pltpu.VMEM(b_key.shape, jnp.bfloat16),
            pltpu.VMEM(b_value.shape, jnp.bfloat16),
            pltpu.VMEM((8, HD), jnp.float32),
            pltpu.VMEM(lists.shape, jnp.int32),
            pltpu.SMEM((2,) + lists.shape, jnp.int32),
            dma((CHUNKS,)),
            dma((CHUNKS, 8)),
            dma((8,)),
            dma((CHUNKS,)),
            dma((CHUNKS,)),
            dma((CHUNKS,)),
            dma((6,)),
            dma((6,)),
            dma((4,)),
            dma((15,)),
            dma((15,)),
            dma((10,)),
            dma((2,)),
            dma((1,)),
            dma((1,)),
        ],
        compiler_params=pltpu.CompilerParams(
            collective_id=0, has_side_effects=True, vmem_limit_bytes=58 << 20
        ),
        name="gather_attend",
    )(
        start_position,
        tokens,
        w_query,
        w_key,
        w_value,
        cache_keys,
        cache_values,
        lists,
        norm_gain,
        b_query,
        b_key,
        b_value,
        table,
    )
    return pl.pallas_call(
        write_kernel,
        out_shape=(
            jax.ShapeDtypeStruct((rows, 20 * HD), jnp.float32),
            jax.ShapeDtypeStruct((rows, 4 * HD), jnp.float32),
            jax.ShapeDtypeStruct((rows, 4 * HD), jnp.float32),
        ),
        in_specs=[vmem],
        out_specs=[hbm] * 3,
        scratch_shapes=[dma((28,))],
        compiler_params=pltpu.CompilerParams(vmem_limit_bytes=4 << 20),
        name="write_out",
    )(heads_out)


def solution(mesh):
    in_specs = (
        P(("ctx", "grp"), None),
        P(),
        P("grp", None),
        P("grp", None),
        P("grp", None),
        P(),
        P(),
        P(),
        P("ctx", None),
        P("ctx", None),
        P(None, ("ctx", "grp"), None),
        P(),
    )
    out_specs = (P(("ctx", "grp"), None), P(("ctx", "grp"), None), P(("ctx", "grp"), None))
    return jax.shard_map(
        on_device, mesh=mesh, in_specs=in_specs, out_specs=out_specs, check_vma=False
    )
```

```python
import functools
import math

import jax
import jax.numpy as jnp
import numpy as np
from jax import lax
from jax.experimental import pallas as pl
from jax.experimental.pallas import tpu as pltpu
from jax.sharding import PartitionSpec as P

MESH = pl.DeviceIdType.MESH

HD = 128
GROUP = 5
QBLK = 128
SEL = 4

norm_eps = 1e-06
rope_base = 10000000.0

NX, NY, NZ = 4, 4, 8
CHUNKS = 11
PLACE = (None, 0, 1, 4, 2, 3, 5, 6, 7, 8, 9)

Y_FIRST = (8,)
NEAR = 1
SCHEDULE = (
    ((
        ("own", 0), ("own", 1), ("own", 3), ("own", 4), ("own", 2), ("kv0", 0), ("kv0", 1),
    ), ("N0",)),
    ((
        ("z", 0, 1, 0), ("own", 5), ("z", 3, 1, 0), ("z", 1, 1, 0), ("z", 4, 1, 0),
        ("z", 0, 2, 0), ("kv1", 0), ("z", 2, 1, 0), ("own", 8), ("own", 9),
    ), ("T",)),
    ((
        ("kv2", 0), ("kv1", 1), ("z", 1, 2, 0), ("z", 0, 3, 0), ("z", 5, 1, 0), ("z", 2, 2, 0),
        ("own", 6),
    ), ("N1",)),
    ((
        ("kv3", 0), ("kv2", 1), ("own", 7), ("z", 0, 4, 0), ("z", 3, 2, 0), ("kv3", 1),
        ("z", 1, 3, 0), ("z", 4, 2, 0), ("z", 2, 3, 0), ("z", 6, 1, 0), ("z", 7, 1, 0), ("b0",),
        ("z", 3, 3, 0), ("z", 5, 2, 0), ("z", 1, 4, 0), ("yf", 8), ("z", 2, 4, 0), ("own", 10),
        ("z", 4, 3, 0), ("z", 6, 2, 0), ("z", 3, 4, 0), ("z", 7, 2, 0), ("z", 5, 3, 0),
        ("z", 9, 1, 0), ("kvw",), ("z", 8, 1, 0), ("z", 4, 4, 0), ("y", 1), ("z", 10, 1, 0),
        ("y", 2), ("z", 8, 1, 1),
    ), ("K", 0)),
    ((
        ("z", 5, 4, 0), ("z", 6, 3, 0), ("z", 7, 3, 0), ("z", 9, 2, 0), ("y", 3),
    ), ("P", 0)),
    ((
        ("z", 10, 2, 0), ("z", 8, 2, 0), ("b1",), ("z", 8, 2, 1),
    ), ("A", 0)),
    ((
        ("y", 4), ("z", 7, 4, 0), ("z", 6, 4, 0), ("z", 9, 3, 0), ("y", 5),
    ), ("K", 1)),
    ((
        ("z", 10, 3, 0), ("b2",),
    ), ("P", 3)),
    ((
        ("z", 8, 3, 0), ("z", 8, 3, 1), ("z", 9, 4, 0),
    ), ("A", 3)),
    ((
        ("y", 7), ("y", 6),
    ), ("P", 1)),
    ((
        ("z", 10, 4, 0),
    ), ("A", 1)),
    ((
        ("z", 8, 4, 1), ("z", 8, 4, 0), ("y", 9), ("y", 8),
    ), ("P", 2)),
    ((

    ), ("A", 2)),
    ((
        ("y", 10), ("b3",),
    ), ("P", 4)),
    ((

    ), ("A", 4)),
)
AHEAD = [op[0] == "own" for op in SCHEDULE[0][0] + (("",),)].index(False)


def angle_tables(head_dim):
    half_dim = head_dim // 2
    frequency = rope_base ** (-2.0 * np.arange(half_dim) / head_dim)
    tables = np.stack(
        [np.mod(frequency * 32.0**digit_level, 2.0 * np.pi) for digit_level in range(4)]
    )
    return np.concatenate([tables, tables], axis=1)


def device_of(x, y, z, core):
    return (x * 4 + (y // 2) * 2 + core, (y % 2) * NZ + z)


def kernel(
    start_ref,
    tok_ref,
    wq_ref,
    wk_ref,
    wv_ref,
    ck_ref,
    cv_ref,
    lists_ref,
    gain_hbm,
    bq_hbm,
    bk_hbm,
    bv_hbm,
    table_hbm,
    out_ref,
    wbuf,
    kvbuf,
    tokbuf,
    normed,
    cosine,
    sine,
    qbuf,
    knew,
    vnew,
    ostage,
    gain_ref,
    bias_ref,
    flat_gain,
    flat_bq,
    flat_bk,
    flat_bv,
    table_ref,
    lvmem,
    lsmem,
    load_sem,
    z_recv,
    z_recv_across,
    y_recv,
    z_send,
    y_send,
    x_recv,
    x_send,
    kv_load,
    kv_recv,
    kv_send,
    misc_sem,
    misc_send,
    out_send,
    out_recv,
):
    ctx = lax.axis_index("ctx")
    grp = lax.axis_index("grp")
    core = ctx % 2
    y_hi = (ctx // 2) % 2
    x = ctx // 4
    y_lo = grp // NZ
    z = grp % NZ
    y = y_hi * 2 + y_lo
    rows = tok_ref.shape[0]

    partner = device_of(x, y, z, 1 - core)
    xp = device_of((x + 1) % NX, y, z, core)
    xm = device_of((x + 3) % NX, y, z, core)
    yp = device_of(x, (y + 1) % NY, z, core)
    ym = device_of(x, (y + 3) % NY, z, core)
    zp = device_of(x, y, (z + 1) % NZ, core)
    zm = device_of(x, y, (z + 7) % NZ, core)
    ykv = device_of(x, (y + 3 + 2 * (y % 2)) % NY, z, core)
    yother = device_of(x, (y + 1 + 2 * (y % 2)) % NY, z, core)

    def remote(src, dst, send_sem, recv_sem, device):
        return pltpu.make_async_remote_copy(
            src_ref=src,
            dst_ref=dst,
            send_sem=send_sem,
            recv_sem=recv_sem,
            device_id=device,
            device_id_type=MESH,
        )

    def columns(index):
        return pl.ds(pl.multiple_of(index * HD, HD), HD)

    def slot_of(i):
        return 10 + x if i == 0 else PLACE[i]

    barrier = pltpu.get_barrier_semaphore()
    for device in (partner, xp, xm, yp, ym, zp, zm):
        pl.semaphore_signal(barrier, inc=1, device_id=device, device_id_type=MESH)

    tok_load = pltpu.make_async_copy(tok_ref, tokbuf.at[0], misc_sem.at[0])
    loads = []
    for i in range(CHUNKS):
        place = PLACE[i]
        if i == 0:
            src = wq_ref.at[:, columns(core * 10 + x)]
        elif place < 4:
            ref = wk_ref if place % 2 == 0 else wv_ref
            src = ref.at[:, columns(core * 2 + place // 2)]
        else:
            src = wq_ref.at[:, columns(core * 10 + place)]
        loads.append(pltpu.make_async_copy(src, wbuf.at[slot_of(i), grp], load_sem.at[i]))
    kv_loads = []
    for part in range(4):
        ref = ck_ref if part < 2 else cv_ref
        kv_loads.append(
            pltpu.make_async_copy(
                ref.at[:, columns(core * 2 + part % 2)], kvbuf.at[ctx, part], kv_load.at[part]
            )
        )
    list_load = pltpu.make_async_copy(lists_ref, lsmem.at[0], misc_sem.at[3])
    table_load = pltpu.make_async_copy(table_hbm, table_ref, misc_sem.at[5])
    flat_loads = [
        pltpu.make_async_copy(src, dst, misc_sem.at[6 + n])
        for n, (src, dst) in enumerate(
            (
                (gain_hbm, flat_gain),
                (bq_hbm, flat_bq),
                (bk_hbm, flat_bk),
                (bv_hbm, flat_bv),
            )
        )
    ]
    for copy in kv_loads + loads[:AHEAD] + [tok_load] + flat_loads + [table_load, list_load] + loads[AHEAD:]:
        copy.start()

    pl.semaphore_wait(barrier, 7)

    shard_rows = wbuf.shape[2]
    half = shard_rows // 2

    def send_y(i, slot, shard, distance):
        row = y_lo * NZ + shard
        cut = half - 16 if distance <= NEAR else half
        lower, upper = wbuf.at[slot, row, 0:cut], wbuf.at[slot, row, cut:shard_rows]
        remote(lower, lower, y_send.at[i], y_recv.at[i], ykv).start()
        remote(upper, upper, y_send.at[i], y_recv.at[i], yother).start()

    def send_z(i, slot, distance, line, wait=False):
        base = (y_lo if line == 0 else 1 - y_lo) * NZ
        back = 0 if wait else 1
        rightward = wbuf.at[slot, base + (z + 8 - distance + back) % NZ]
        leftward = wbuf.at[slot, base + (z + distance - back) % NZ]
        if distance == 4:
            rightward, leftward = rightward.at[0:half], leftward.at[half:shard_rows]
        recv = [
            z_recv.at[i, n] if line == 0 else z_recv_across.at[n]
            for n in (distance - 1, 3 + distance)
        ]
        copies = (
            remote(rightward, rightward, z_send.at[i], recv[0], zp),
            remote(leftward, leftward, z_send.at[i], recv[1], zm),
        )
        for copy in copies:
            if wait:
                copy.wait_recv()
            else:
                copy.start()

    def send_own(i):
        slot = slot_of(i)
        loads[i].wait()
        send_z(i, slot, 1, 0)
        send_y(i, slot, z, 0)

    def pass_on(i, distance, line):
        slot = slot_of(i)
        send_z(i, slot, distance, line, wait=True)
        if distance < 4:
            send_z(i, slot, distance + 1, line)
        if i in Y_FIRST:
            return
        send_y(i, slot, (z + 8 - distance) % NZ, distance)
        if distance < 4:
            send_y(i, slot, (z + distance) % NZ, distance)

    def send_across(i):
        slot = slot_of(i)
        landed = wbuf.at[slot, (1 - y_lo) * NZ + z]
        remote(landed, landed, y_send.at[i], y_recv.at[i], ykv).wait_recv()
        send_z(i, slot, 1, 1)

    def wait_y(i):
        if i in Y_FIRST:
            return
        landed = wbuf.at[slot_of(i), pl.ds((1 - y_lo) * NZ, NZ)]
        remote(landed, landed, y_send.at[i], y_recv.at[i], ykv).wait_recv()

    kv_parts = []
    for part in range(4):
        ref = ck_ref if part < 2 else cv_ref
        kv_parts.append(
            remote(
                ref.at[:, columns((1 - core) * 2 + part % 2)],
                kvbuf.at[ctx, part],
                kv_send.at[0],
                kv_recv.at[0],
                partner,
            )
        )

    def cached(at_x, at_y, side):
        return kvbuf.at[at_x * 4 + at_y * 2 + (core if side == 0 else 1 - core)]

    left_x, right_x, far_x = (x + 3) % NX, (x + 1) % NX, (x + 2) % NX

    def kv_copy(number, side):
        at_x, at_y, device = (
            (x, y_hi, ykv),
            (x, y_hi, xp),
            (x, y_hi, xm),
            (x, 1 - y_hi, xp),
            (x, 1 - y_hi, xm),
            (left_x, y_hi, xp),
            (right_x, 1 - y_hi, xm),
        )[number]
        block = cached(at_x, at_y, side)
        number = 1 + 7 * side + number
        return remote(block, block, kv_send.at[number], kv_recv.at[number], device)

    def shared(at_x, upper):
        return wbuf.at[10 + at_x, 8:16] if upper else wbuf.at[10 + at_x, 0:8]

    x_copies = [
        remote(shared(x, 0), shared(x, 0), x_send.at[0], x_recv.at[0], xp),
        remote(shared(x, 1), shared(x, 1), x_send.at[1], x_recv.at[1], xm),
        remote(shared(x, 1), shared(x, 1), x_send.at[2], x_recv.at[2], xp),
        remote(shared(x, 0), shared(x, 0), x_send.at[3], x_recv.at[3], xm),
        remote(shared(left_x, 0), shared(left_x, 0), x_send.at[4], x_recv.at[4], xp),
        remote(shared(right_x, 1), shared(right_x, 1), x_send.at[5], x_recv.at[5], xm),
    ]

    def norm_rows(part):
        @pl.loop(0, rows // 64)
        def _(step):
            at = pl.ds(pl.multiple_of(step * 64, 64), 64)
            wide = tokbuf[part, at, :].astype(jnp.float32)
            mean = jnp.mean(wide * wide, axis=-1, keepdims=True)
            scaled = wide * lax.rsqrt(mean + norm_eps) * gain_ref[0:1, :]
            normed[pl.ds(pl.multiple_of(part * rows + step * 64, 64), 64), :] = scaled.astype(
                jnp.bfloat16
            )

    def tables():
        lane = lax.broadcasted_iota(jnp.int32, (QBLK, HD), 1)
        sign = jnp.where(lane < HD // 2, -1.0, 1.0)

        @pl.loop(0, 2 * rows // QBLK)
        def _(step):
            of_ctx = jnp.where(step < rows // QBLK, ctx, ctx + 1 - 2 * core)
            first = (of_ctx * 16 + grp) * rows + (step % (rows // QBLK)) * QBLK
            position = start_ref[0] + first + lax.broadcasted_iota(jnp.int32, (QBLK, HD), 0)
            angle = jnp.zeros((QBLK, HD), jnp.float32)
            for level in range(4):
                digit = ((position >> (5 * level)) & 31).astype(jnp.float32)
                angle = angle + digit * table_ref[level : level + 1, :]
            turns = jnp.floor(angle * (1.0 / (2.0 * math.pi)) + 0.5)
            angle = (angle - turns * 6.28125) - turns * (2.0 * math.pi - 6.28125)
            at = pl.ds(pl.multiple_of(step * QBLK, QBLK), QBLK)
            cosine[at, :] = jnp.cos(angle)
            sine[at, :] = jnp.sin(angle) * sign

    def project(slots, bias_rows):
        weights = [wbuf[slot].reshape(normed.shape[1], HD) for slot in slots]
        linear = jnp.dot(
            normed[...], jnp.concatenate(weights, axis=1), preferred_element_type=jnp.float32
        )
        return [
            linear[:, n * HD : (n + 1) * HD] + bias_ref[pl.ds(row, 1), :]
            for n, row in enumerate(bias_rows)
        ]

    def rope(linear):
        return linear * cosine[...] + pltpu.roll(linear, HD // 2, 1) * sine[...]

    def copy_out(slot, place):
        other, target = ostage.at[slot], out_ref.at[:, columns(place)]
        remote(other, target, out_send.at[0], out_recv.at[0], partner).start()

    def key_value_chunks(head):
        global_head = core * 2 + head
        linear_key, linear_value = project(
            (2 * head, 2 * head + 1), (20 + global_head, 24 + global_head)
        )
        key = rope(linear_key)
        knew[head] = key.astype(jnp.bfloat16)
        ostage[2 * head] = key[rows:]
        copy_out(2 * head, 20 + global_head)
        out_ref[:, columns(20 + global_head)] = key[:rows]
        vnew[head] = linear_value.astype(jnp.bfloat16)
        ostage[2 * head + 1] = linear_value[rows:]
        copy_out(2 * head + 1, 24 + global_head)
        out_ref[:, columns(24 + global_head)] = linear_value[:rows]

    scale = HD**-0.5 * math.log2(math.e)
    row_at = lax.broadcasted_iota(jnp.int32, (QBLK, QBLK), 0)
    column_at = lax.broadcasted_iota(jnp.int32, (QBLK, QBLK), 1)
    blocks = rows // QBLK

    def attend(slots):
        todo = [(n, block) for n in range(2) for block in range(2 * blocks)]
        scores, values = {}, {}
        for n, block in todo:
            local = slots[n] % 10
            head = local // GROUP
            at = slice(block * QBLK, (block + 1) * QBLK)
            keys, shifts = [], []
            values[n, block] = []
            for step in range(SEL):
                index = lsmem[block // blocks, block % blocks, step, core * 10 + local]
                shifts.append(jnp.where(index >= 0, 0.0, -jnp.inf))
                index = jnp.maximum(index, 0)
                keys.append(kvbuf[index, head])
                values[n, block].append(kvbuf[index, 2 + head])
            keys.append(knew[head, at, :])
            values[n, block].append(vnew[head, at, :])
            all_keys = lax.dot_general(
                qbuf[n, at, :],
                jnp.concatenate(keys, axis=0),
                (((1,), (1,)), ((), ())),
                preferred_element_type=jnp.float32,
            )
            parts = [
                all_keys[:, step * QBLK : (step + 1) * QBLK] + shifts[step] for step in range(SEL)
            ]
            near = all_keys[:, SEL * QBLK :]
            scores[n, block] = parts + [jnp.where(row_at >= column_at, near, -jnp.inf)]
        largest = {
            at: jnp.max(functools.reduce(jnp.maximum, scores[at]), axis=1, keepdims=True)
            for at in todo
        }
        for n, block in sorted(todo, key=lambda at: (at[1] < blocks, at)):
            weights = [jnp.exp2(part - largest[n, block]) for part in scores[n, block]]
            total = jnp.sum(functools.reduce(jnp.add, weights), axis=1, keepdims=True)
            mixed = jnp.dot(
                jnp.concatenate([part.astype(jnp.bfloat16) for part in weights], axis=1),
                jnp.concatenate(values[n, block], axis=0),
                preferred_element_type=jnp.float32,
            )
            result = mixed * (1.0 / total)
            place = core * 10 + slots[n] % 10
            at = slice(block % blocks * QBLK, (block % blocks + 1) * QBLK)
            if block >= blocks:
                ostage[slots[n], at, :] = result
            else:
                out_ref[at, columns(place)] = result
            if block == 2 * blocks - 1:
                copy_out(slots[n], place)

    def query_chunks(first, second):
        heads = (core * 10 + first % 10, core * 10 + second % 10)
        linear = project((first, second), heads)
        for n in range(2):
            qbuf[n] = (rope(linear[n]) * scale).astype(jnp.bfloat16)

    tok_send = remote(tok_ref, tokbuf.at[1], misc_send.at[0], misc_sem.at[1], partner)
    list_send = remote(lists_ref, lvmem, misc_send.at[1], misc_sem.at[2], partner)

    def kv_wait(landed, number, side):
        number = 1 + 7 * side + number
        remote(landed, landed, kv_send.at[number], kv_recv.at[number], xp).wait_recv()

    def shared_wait(landed, number):
        remote(landed, landed, x_send.at[number], x_recv.at[number], xp).wait_recv()

    def run(op):
        kind, at = op[0], op[1:]
        if kind == "own":
            send_own(*at)
        elif kind == "z":
            pass_on(*at)
        elif kind == "yf":
            send_across(*at)
        elif kind == "y":
            wait_y(*at)
        elif kind == "kv0":
            if at[0] == 0:
                for copy in kv_loads:
                    copy.wait()
            else:
                other = kvbuf.at[ctx + 1 - 2 * core]
                remote(other, other, kv_send.at[0], kv_recv.at[0], partner).wait_recv()
            for number in range(3):
                kv_copy(number, at[0]).start()
        elif kind == "kv1":
            kv_wait(cached(x, 1 - y_hi, at[0]), 0, at[0])
            kv_copy(3, at[0]).start()
            kv_copy(4, at[0]).start()
        elif kind == "kv2":
            kv_wait(cached(left_x, y_hi, at[0]), 1, at[0])
            kv_copy(5, at[0]).start()
        elif kind == "kv3":
            kv_wait(cached(right_x, 1 - y_hi, at[0]), 4, at[0])
            kv_copy(6, at[0]).start()
        elif kind == "kvw":
            for side in range(2):
                kv_wait(cached(right_x, y_hi, side), 2, side)
                kv_wait(cached(left_x, 1 - y_hi, side), 3, side)
                kv_wait(cached(far_x, y_hi, side), 5, side)
                kv_wait(cached(far_x, 1 - y_hi, side), 6, side)
        elif kind == "b0":
            wait_y(0)
            for copy in x_copies[:4]:
                copy.start()
        elif kind == "b1":
            shared_wait(shared(left_x, 0), 0)
            shared_wait(shared(right_x, 1), 1)
            x_copies[4].start()
            x_copies[5].start()
        elif kind == "b2":
            shared_wait(shared(left_x, 1), 2)
            shared_wait(shared(right_x, 0), 3)
        elif kind == "b3":
            shared_wait(shared(far_x, 0), 4)
            shared_wait(shared(far_x, 1), 5)

    for copy in kv_parts:
        copy.start()
    for op in SCHEDULE[0][0][:AHEAD]:
        run(op)
    list_send.start()
    tok_send.start()
    table_load.wait()
    for copy in flat_loads:
        copy.wait()
    gain_ref[0:1, :] = flat_gain[...].astype(jnp.float32).reshape(1, gain_ref.shape[1])
    row = 0
    for flat in (flat_bq, flat_bk, flat_bv):
        for step in range(flat.shape[0] // HD):
            piece = flat[step * HD : (step + 1) * HD].astype(jnp.float32)
            bias_ref[row : row + 1, :] = piece.reshape(1, HD)
            row += 1

    pairs = (
        (10 + x, 4),
        (5, 6),
        (7, 8),
        (10 + left_x, 10 + right_x),
        (9, 10 + far_x),
    )
    units = [unit for _, unit in SCHEDULE]

    @pl.loop(0, len(SCHEDULE))
    def _(now):
        for number, (ops, _unused) in enumerate(SCHEDULE):
            rest = ops[AHEAD:] if number == 0 else ops
            if rest:

                @pl.when(now == number)
                def _():
                    for op in rest:
                        run(op)

        def on(kind):
            places = [n for n, unit in enumerate(units) if unit[0] == kind]
            condition = functools.reduce(jnp.logical_or, [now == n for n in places])

            def pick(values):
                value = values[units[places[-1]][1]]
                for n in places[:-1]:
                    value = jnp.where(now == n, values[units[n][1]], value)
                return value

            return condition, pick

        @pl.when(on("N0")[0])
        def _():
            tok_load.wait()
            norm_rows(0)

        @pl.when(on("T")[0])
        def _():
            tables()

        @pl.when(on("N1")[0])
        def _():
            tok_send.wait_recv()
            norm_rows(1)
            list_send.wait_recv()
            list_load.wait()
            move = pltpu.make_async_copy(lvmem, lsmem.at[1], misc_sem.at[4])
            move.start()
            move.wait()

        condition, pick_pair = on("K")

        @pl.when(condition)
        def _():
            key_value_chunks(pick_pair((0, 1)))

        condition, pick_query = on("P")

        @pl.when(condition)
        def _():
            query_chunks(
                pick_query([first for first, _ in pairs]),
                pick_query([second for _, second in pairs]),
            )

        condition, pick_heads = on("A")

        @pl.when(condition)
        def _():
            attend(
                (
                    pick_heads([first for first, _ in pairs]),
                    pick_heads([second for _, second in pairs]),
                )
            )

    for i in range(CHUNKS):
        sent = wbuf.at[0, 0:14] if i in Y_FIRST else wbuf.at[0, 0:7]
        pltpu.make_async_copy(sent, sent, z_send.at[i]).wait()
        sent = wbuf.at[0, 0] if i in Y_FIRST else wbuf.at[0, 0:8]
        pltpu.make_async_copy(sent, sent, y_send.at[i]).wait()

    for copy in x_copies:
        copy.wait_send()
    pltpu.make_async_copy(kvbuf.at[0], kvbuf.at[0], kv_send.at[0]).wait()
    for side in range(2):
        for number in range(7):
            kv_copy(number, side).wait_send()
    tok_send.wait_send()
    list_send.wait_send()
    written = ostage
    pltpu.make_async_copy(written, written, out_send.at[0]).wait()
    pltpu.make_async_copy(written, written, out_recv.at[0]).wait()


def write_kernel(source, ctx_ref, keys_ref, values_ref, sem):
    copies = []
    rows = source.shape[0] // 4
    for part in range(4):
        at = slice(part * rows, (part + 1) * rows)
        for n, (target, first) in enumerate(((ctx_ref, 0), (keys_ref, 20), (values_ref, 24))):
            column = slice(first * HD, first * HD + target.shape[1])
            copies.append(
                pltpu.make_async_copy(
                    source.at[at, column], target.at[at, :], sem.at[part * 3 + n]
                )
            )
    for copy in copies:
        copy.start()
    for copy in copies:
        copy.wait()


def on_device(
    tokens,
    norm_gain,
    w_query,
    w_key,
    w_value,
    b_query,
    b_key,
    b_value,
    cache_keys,
    cache_values,
    block_lists,
    start_position,
):
    rows, features = tokens.shape
    shard = w_query.shape[0]
    lists = jnp.transpose(block_lists, (1, 2, 0))
    table = jnp.asarray(np.pad(angle_tables(HD), ((0, 4), (0, 0))), jnp.float32)
    hbm = pl.BlockSpec(memory_space=pltpu.HBM)
    vmem = pl.BlockSpec(memory_space=pltpu.VMEM)
    smem = pl.BlockSpec(memory_space=pltpu.SMEM)
    dma = pltpu.SemaphoreType.DMA
    heads_out = pl.pallas_call(
        kernel,
        out_shape=pltpu.VMEM((rows, 28 * HD), jnp.float32),
        in_specs=[smem] + [hbm] * 12,
        out_specs=pl.BlockSpec(memory_space=pltpu.VMEM),
        scratch_shapes=[
            pltpu.VMEM((14, 16, shard, HD), jnp.bfloat16),
            pltpu.VMEM((16, 4, QBLK, HD), jnp.bfloat16),
            pltpu.VMEM((2, rows, features), jnp.bfloat16),
            pltpu.VMEM((2 * rows, features), jnp.bfloat16),
            pltpu.VMEM((2 * rows, HD), jnp.float32),
            pltpu.VMEM((2 * rows, HD), jnp.float32),
            pltpu.VMEM((2, 2 * rows, HD), jnp.bfloat16),
            pltpu.VMEM((2, 2 * rows, HD), jnp.bfloat16),
            pltpu.VMEM((2, 2 * rows, HD), jnp.bfloat16),
            pltpu.VMEM((14, rows, HD), jnp.float32),
            pltpu.VMEM((8, features), jnp.float32),
            pltpu.VMEM((32, HD), jnp.float32),
            pltpu.VMEM(norm_gain.shape, jnp.bfloat16),
            pltpu.VMEM(b_query.shape, jnp.bfloat16),
            pltpu.VMEM(b_key.shape, jnp.bfloat16),
            pltpu.VMEM(b_value.shape, jnp.bfloat16),
            pltpu.VMEM((8, HD), jnp.float32),
            pltpu.VMEM(lists.shape, jnp.int32),
            pltpu.SMEM((2,) + lists.shape, jnp.int32),
            dma((CHUNKS,)),
            dma((CHUNKS, 8)),
            dma((8,)),
            dma((CHUNKS,)),
            dma((CHUNKS,)),
            dma((CHUNKS,)),
            dma((6,)),
            dma((6,)),
            dma((4,)),
            dma((15,)),
            dma((15,)),
            dma((10,)),
            dma((2,)),
            dma((1,)),
            dma((1,)),
        ],
        compiler_params=pltpu.CompilerParams(
            collective_id=0, has_side_effects=True, vmem_limit_bytes=58 << 20
        ),
        name="gather_attend",
    )(
        start_position,
        tokens,
        w_query,
        w_key,
        w_value,
        cache_keys,
        cache_values,
        lists,
        norm_gain,
        b_query,
        b_key,
        b_value,
        table,
    )
    return pl.pallas_call(
        write_kernel,
        out_shape=(
            jax.ShapeDtypeStruct((rows, 20 * HD), jnp.float32),
            jax.ShapeDtypeStruct((rows, 4 * HD), jnp.float32),
            jax.ShapeDtypeStruct((rows, 4 * HD), jnp.float32),
        ),
        in_specs=[vmem],
        out_specs=[hbm] * 3,
        scratch_shapes=[dma((12,))],
        compiler_params=pltpu.CompilerParams(vmem_limit_bytes=4 << 20),
        name="write_out",
    )(heads_out)


def solution(mesh):
    in_specs = (
        P(("ctx", "grp"), None),
        P(),
        P("grp", None),
        P("grp", None),
        P("grp", None),
        P(),
        P(),
        P(),
        P("ctx", None),
        P("ctx", None),
        P(None, ("ctx", "grp"), None),
        P(),
    )
    out_specs = (P(("ctx", "grp"), None), P(("ctx", "grp"), None), P(("ctx", "grp"), None))
    return jax.shard_map(
        on_device, mesh=mesh, in_specs=in_specs, out_specs=out_specs, check_vma=False
    )
```

```python
import functools
import math

import jax
import jax.numpy as jnp
import numpy as np
from jax import lax
from jax.experimental import pallas as pl
from jax.experimental.pallas import tpu as pltpu
from jax.sharding import PartitionSpec as P

MESH = pl.DeviceIdType.MESH

HD = 128
GROUP = 5
QBLK = 128
SEL = 4

norm_eps = 1e-06
rope_base = 10000000.0

NX, NY, NZ = 4, 4, 8
CHUNKS = 11
PLACE = (None, 0, 1, 4, 2, 3, 5, 6, 7, 8, 9)

Y_FIRST = (8,)
NEAR = 1
SCHEDULE = (
    ((
        ("own", 0), ("own", 1), ("own", 3), ("own", 4), ("own", 2), ("kv0", 0), ("kv0", 1),
    ), ("N0",)),
    ((
        ("z", 0, 1, 0), ("own", 5), ("z", 3, 1, 0), ("z", 1, 1, 0), ("z", 4, 1, 0),
        ("z", 0, 2, 0), ("kv1", 0), ("z", 2, 1, 0), ("own", 8), ("own", 9),
    ), ("T",)),
    ((
        ("kv2", 0), ("kv1", 1), ("z", 1, 2, 0), ("z", 0, 3, 0), ("z", 5, 1, 0), ("z", 2, 2, 0),
        ("own", 6),
    ), ("N1",)),
    ((
        ("kv3", 0), ("kv2", 1), ("own", 7), ("z", 0, 4, 0), ("z", 3, 2, 0), ("kv3", 1),
        ("z", 1, 3, 0), ("z", 4, 2, 0), ("z", 2, 3, 0), ("z", 6, 1, 0), ("z", 7, 1, 0), ("b0",),
        ("z", 3, 3, 0), ("z", 5, 2, 0), ("z", 1, 4, 0), ("yf", 8), ("z", 2, 4, 0), ("own", 10),
        ("z", 4, 3, 0), ("z", 6, 2, 0), ("z", 3, 4, 0), ("z", 7, 2, 0), ("z", 5, 3, 0),
        ("z", 9, 1, 0), ("kvw",), ("z", 8, 1, 0), ("z", 4, 4, 0), ("y", 1), ("z", 10, 1, 0),
        ("y", 2), ("z", 8, 1, 1),
    ), ("K", 0)),
    ((
        ("z", 5, 4, 0), ("z", 6, 3, 0), ("z", 7, 3, 0), ("z", 9, 2, 0), ("y", 3),
    ), ("P", 0)),
    ((
        ("z", 10, 2, 0), ("z", 8, 2, 0), ("b1",), ("z", 8, 2, 1),
    ), ("A", 0)),
    ((
        ("y", 4), ("z", 7, 4, 0), ("z", 6, 4, 0), ("z", 9, 3, 0), ("y", 5),
    ), ("K", 1)),
    ((
        ("z", 10, 3, 0), ("b2",),
    ), ("P", 3)),
    ((
        ("z", 8, 3, 0), ("z", 8, 3, 1), ("z", 9, 4, 0), ("y", 7), ("y", 6),
    ), ("X", 0)),
    ((
        ("z", 10, 4, 0),
    ), ("A", 1)),
    ((
        ("z", 8, 4, 1), ("z", 8, 4, 0), ("y", 9), ("y", 8),
    ), ("P", 2)),
    ((

    ), ("A", 2)),
    ((
        ("y", 10), ("b3",),
    ), ("P", 4)),
    ((

    ), ("A", 4)),
)
AHEAD = [op[0] == "own" for op in SCHEDULE[0][0] + (("",),)].index(False)


def angle_tables(head_dim):
    half_dim = head_dim // 2
    frequency = rope_base ** (-2.0 * np.arange(half_dim) / head_dim)
    tables = np.stack(
        [np.mod(frequency * 32.0**digit_level, 2.0 * np.pi) for digit_level in range(4)]
    )
    return np.concatenate([tables, tables], axis=1)


def device_of(x, y, z, core):
    return (x * 4 + (y // 2) * 2 + core, (y % 2) * NZ + z)


def kernel(
    start_ref,
    tok_ref,
    wq_ref,
    wk_ref,
    wv_ref,
    ck_ref,
    cv_ref,
    lists_ref,
    gain_hbm,
    bq_hbm,
    bk_hbm,
    bv_hbm,
    table_hbm,
    out_ref,
    wbuf,
    kvbuf,
    tokbuf,
    normed,
    cosine,
    sine,
    qbuf,
    knew,
    vnew,
    ostage,
    gain_ref,
    bias_ref,
    flat_gain,
    flat_bq,
    flat_bk,
    flat_bv,
    table_ref,
    lvmem,
    lsmem,
    load_sem,
    z_recv,
    z_recv_across,
    y_recv,
    z_send,
    y_send,
    x_recv,
    x_send,
    kv_load,
    kv_recv,
    kv_send,
    misc_sem,
    misc_send,
    out_send,
    out_recv,
):
    ctx = lax.axis_index("ctx")
    grp = lax.axis_index("grp")
    core = ctx % 2
    y_hi = (ctx // 2) % 2
    x = ctx // 4
    y_lo = grp // NZ
    z = grp % NZ
    y = y_hi * 2 + y_lo
    rows = tok_ref.shape[0]

    partner = device_of(x, y, z, 1 - core)
    xp = device_of((x + 1) % NX, y, z, core)
    xm = device_of((x + 3) % NX, y, z, core)
    yp = device_of(x, (y + 1) % NY, z, core)
    ym = device_of(x, (y + 3) % NY, z, core)
    zp = device_of(x, y, (z + 1) % NZ, core)
    zm = device_of(x, y, (z + 7) % NZ, core)
    ykv = device_of(x, (y + 3 + 2 * (y % 2)) % NY, z, core)
    yother = device_of(x, (y + 1 + 2 * (y % 2)) % NY, z, core)

    def remote(src, dst, send_sem, recv_sem, device):
        return pltpu.make_async_remote_copy(
            src_ref=src,
            dst_ref=dst,
            send_sem=send_sem,
            recv_sem=recv_sem,
            device_id=device,
            device_id_type=MESH,
        )

    def columns(index):
        return pl.ds(pl.multiple_of(index * HD, HD), HD)

    def slot_of(i):
        return 10 + x if i == 0 else PLACE[i]

    barrier = pltpu.get_barrier_semaphore()
    for device in (partner, xp, xm, yp, ym, zp, zm):
        pl.semaphore_signal(barrier, inc=1, device_id=device, device_id_type=MESH)

    tok_load = pltpu.make_async_copy(tok_ref, tokbuf.at[0], misc_sem.at[0])
    loads = []
    for i in range(CHUNKS):
        place = PLACE[i]
        if i == 0:
            src = wq_ref.at[:, columns(core * 10 + x)]
        elif place < 4:
            ref = wk_ref if place % 2 == 0 else wv_ref
            src = ref.at[:, columns(core * 2 + place // 2)]
        else:
            src = wq_ref.at[:, columns(core * 10 + place)]
        loads.append(pltpu.make_async_copy(src, wbuf.at[slot_of(i), grp], load_sem.at[i]))
    kv_loads = []
    for part in range(4):
        ref = ck_ref if part < 2 else cv_ref
        kv_loads.append(
            pltpu.make_async_copy(
                ref.at[:, columns(core * 2 + part % 2)], kvbuf.at[ctx, part], kv_load.at[part]
            )
        )
    list_load = pltpu.make_async_copy(lists_ref, lsmem.at[0], misc_sem.at[3])
    table_load = pltpu.make_async_copy(table_hbm, table_ref, misc_sem.at[5])
    flat_loads = [
        pltpu.make_async_copy(src, dst, misc_sem.at[6 + n])
        for n, (src, dst) in enumerate(
            (
                (gain_hbm, flat_gain),
                (bq_hbm, flat_bq),
                (bk_hbm, flat_bk),
                (bv_hbm, flat_bv),
            )
        )
    ]
    for copy in kv_loads + loads[:AHEAD] + [tok_load] + flat_loads + [table_load, list_load] + loads[AHEAD:]:
        copy.start()

    pl.semaphore_wait(barrier, 7)

    shard_rows = wbuf.shape[2]
    half = shard_rows // 2

    def send_y(i, slot, shard, distance):
        row = y_lo * NZ + shard
        cut = half - 16 if distance <= NEAR else half
        lower, upper = wbuf.at[slot, row, 0:cut], wbuf.at[slot, row, cut:shard_rows]
        remote(lower, lower, y_send.at[i], y_recv.at[i], ykv).start()
        remote(upper, upper, y_send.at[i], y_recv.at[i], yother).start()

    def send_z(i, slot, distance, line, wait=False):
        base = (y_lo if line == 0 else 1 - y_lo) * NZ
        back = 0 if wait else 1
        rightward = wbuf.at[slot, base + (z + 8 - distance + back) % NZ]
        leftward = wbuf.at[slot, base + (z + distance - back) % NZ]
        if distance == 4:
            rightward, leftward = rightward.at[0:half], leftward.at[half:shard_rows]
        recv = [
            z_recv.at[i, n] if line == 0 else z_recv_across.at[n]
            for n in (distance - 1, 3 + distance)
        ]
        copies = (
            remote(rightward, rightward, z_send.at[i], recv[0], zp),
            remote(leftward, leftward, z_send.at[i], recv[1], zm),
        )
        for copy in copies:
            if wait:
                copy.wait_recv()
            else:
                copy.start()

    def send_own(i):
        slot = slot_of(i)
        loads[i].wait()
        send_z(i, slot, 1, 0)
        send_y(i, slot, z, 0)

    def pass_on(i, distance, line):
        slot = slot_of(i)
        send_z(i, slot, distance, line, wait=True)
        if distance < 4:
            send_z(i, slot, distance + 1, line)
        if i in Y_FIRST:
            return
        send_y(i, slot, (z + 8 - distance) % NZ, distance)
        if distance < 4:
            send_y(i, slot, (z + distance) % NZ, distance)

    def send_across(i):
        slot = slot_of(i)
        landed = wbuf.at[slot, (1 - y_lo) * NZ + z]
        remote(landed, landed, y_send.at[i], y_recv.at[i], ykv).wait_recv()
        send_z(i, slot, 1, 1)

    def wait_y(i):
        if i in Y_FIRST:
            return
        landed = wbuf.at[slot_of(i), pl.ds((1 - y_lo) * NZ, NZ)]
        remote(landed, landed, y_send.at[i], y_recv.at[i], ykv).wait_recv()

    kv_parts = []
    for part in range(4):
        ref = ck_ref if part < 2 else cv_ref
        kv_parts.append(
            remote(
                ref.at[:, columns((1 - core) * 2 + part % 2)],
                kvbuf.at[ctx, part],
                kv_send.at[0],
                kv_recv.at[0],
                partner,
            )
        )

    def cached(at_x, at_y, side):
        return kvbuf.at[at_x * 4 + at_y * 2 + (core if side == 0 else 1 - core)]

    left_x, right_x, far_x = (x + 3) % NX, (x + 1) % NX, (x + 2) % NX

    def kv_copy(number, side):
        at_x, at_y, device = (
            (x, y_hi, ykv),
            (x, y_hi, xp),
            (x, y_hi, xm),
            (x, 1 - y_hi, xp),
            (x, 1 - y_hi, xm),
            (left_x, y_hi, xp),
            (right_x, 1 - y_hi, xm),
        )[number]
        block = cached(at_x, at_y, side)
        number = 1 + 7 * side + number
        return remote(block, block, kv_send.at[number], kv_recv.at[number], device)

    def shared(at_x, upper):
        return wbuf.at[10 + at_x, 8:16] if upper else wbuf.at[10 + at_x, 0:8]

    x_copies = [
        remote(shared(x, 0), shared(x, 0), x_send.at[0], x_recv.at[0], xp),
        remote(shared(x, 1), shared(x, 1), x_send.at[1], x_recv.at[1], xm),
        remote(shared(x, 1), shared(x, 1), x_send.at[2], x_recv.at[2], xp),
        remote(shared(x, 0), shared(x, 0), x_send.at[3], x_recv.at[3], xm),
        remote(shared(left_x, 0), shared(left_x, 0), x_send.at[4], x_recv.at[4], xp),
        remote(shared(right_x, 1), shared(right_x, 1), x_send.at[5], x_recv.at[5], xm),
    ]

    def norm_rows(part):
        @pl.loop(0, rows // 64)
        def _(step):
            at = pl.ds(pl.multiple_of(step * 64, 64), 64)
            wide = tokbuf[part, at, :].astype(jnp.float32)
            mean = jnp.mean(wide * wide, axis=-1, keepdims=True)
            scaled = wide * lax.rsqrt(mean + norm_eps) * gain_ref[0:1, :]
            normed[pl.ds(pl.multiple_of(part * rows + step * 64, 64), 64), :] = scaled.astype(
                jnp.bfloat16
            )

    def tables():
        lane = lax.broadcasted_iota(jnp.int32, (QBLK, HD), 1)
        sign = jnp.where(lane < HD // 2, -1.0, 1.0)

        @pl.loop(0, 2 * rows // QBLK)
        def _(step):
            of_ctx = jnp.where(step < rows // QBLK, ctx, ctx + 1 - 2 * core)
            first = (of_ctx * 16 + grp) * rows + (step % (rows // QBLK)) * QBLK
            position = start_ref[0] + first + lax.broadcasted_iota(jnp.int32, (QBLK, HD), 0)
            angle = jnp.zeros((QBLK, HD), jnp.float32)
            for level in range(4):
                digit = ((position >> (5 * level)) & 31).astype(jnp.float32)
                angle = angle + digit * table_ref[level : level + 1, :]
            turns = jnp.floor(angle * (1.0 / (2.0 * math.pi)) + 0.5)
            angle = (angle - turns * 6.28125) - turns * (2.0 * math.pi - 6.28125)
            at = pl.ds(pl.multiple_of(step * QBLK, QBLK), QBLK)
            cosine[at, :] = jnp.cos(angle)
            sine[at, :] = jnp.sin(angle) * sign

    def project(slots, bias_rows):
        weights = [wbuf[slot].reshape(normed.shape[1], HD) for slot in slots]
        linear = jnp.dot(
            normed[...], jnp.concatenate(weights, axis=1), preferred_element_type=jnp.float32
        )
        return [
            linear[:, n * HD : (n + 1) * HD] + bias_ref[pl.ds(row, 1), :]
            for n, row in enumerate(bias_rows)
        ]

    def rope(linear):
        return linear * cosine[...] + pltpu.roll(linear, HD // 2, 1) * sine[...]

    def copy_out(slot, place):
        other, target = ostage.at[slot], out_ref.at[:, columns(place)]
        remote(other, target, out_send.at[0], out_recv.at[0], partner).start()

    def key_value_chunks(head):
        global_head = core * 2 + head
        linear_key, linear_value = project(
            (2 * head, 2 * head + 1), (20 + global_head, 24 + global_head)
        )
        key = rope(linear_key)
        knew[head] = key.astype(jnp.bfloat16)
        ostage[2 * head] = key[rows:]
        copy_out(2 * head, 20 + global_head)
        out_ref[:, columns(20 + global_head)] = key[:rows]
        vnew[head] = linear_value.astype(jnp.bfloat16)
        ostage[2 * head + 1] = linear_value[rows:]
        copy_out(2 * head + 1, 24 + global_head)
        out_ref[:, columns(24 + global_head)] = linear_value[:rows]

    scale = HD**-0.5 * math.log2(math.e)
    row_at = lax.broadcasted_iota(jnp.int32, (QBLK, QBLK), 0)
    column_at = lax.broadcasted_iota(jnp.int32, (QBLK, QBLK), 1)
    blocks = rows // QBLK

    def attend(slots, base):
        todo = [(n, block) for n in range(2) for block in range(2 * blocks)]
        scores, values = {}, {}
        for n, block in todo:
            local = slots[n] % 10
            head = local // GROUP
            at = slice(block * QBLK, (block + 1) * QBLK)
            keys, shifts = [], []
            values[n, block] = []
            for step in range(SEL):
                index = lsmem[block // blocks, block % blocks, step, core * 10 + local]
                shifts.append(jnp.where(index >= 0, 0.0, -jnp.inf))
                index = jnp.maximum(index, 0)
                keys.append(kvbuf[index, head])
                values[n, block].append(kvbuf[index, 2 + head])
            keys.append(knew[head, at, :])
            values[n, block].append(vnew[head, at, :])
            all_keys = lax.dot_general(
                qbuf[base + n, at, :],
                jnp.concatenate(keys, axis=0),
                (((1,), (1,)), ((), ())),
                preferred_element_type=jnp.float32,
            )
            parts = [
                all_keys[:, step * QBLK : (step + 1) * QBLK] + shifts[step] for step in range(SEL)
            ]
            near = all_keys[:, SEL * QBLK :]
            scores[n, block] = parts + [jnp.where(row_at >= column_at, near, -jnp.inf)]
        largest = {
            at: jnp.max(functools.reduce(jnp.maximum, scores[at]), axis=1, keepdims=True)
            for at in todo
        }
        for n, block in sorted(todo, key=lambda at: (at[1] < blocks, at)):
            weights = [jnp.exp2(part - largest[n, block]) for part in scores[n, block]]
            total = jnp.sum(functools.reduce(jnp.add, weights), axis=1, keepdims=True)
            mixed = jnp.dot(
                jnp.concatenate([part.astype(jnp.bfloat16) for part in weights], axis=1),
                jnp.concatenate(values[n, block], axis=0),
                preferred_element_type=jnp.float32,
            )
            result = mixed * (1.0 / total)
            place = core * 10 + slots[n] % 10
            at = slice(block % blocks * QBLK, (block % blocks + 1) * QBLK)
            if block >= blocks:
                ostage[slots[n], at, :] = result
            else:
                out_ref[at, columns(place)] = result
            if block == 2 * blocks - 1:
                copy_out(slots[n], place)

    def query_chunks(first, second, base):
        heads = (core * 10 + first % 10, core * 10 + second % 10)
        linear = project((first, second), heads)
        for n in range(2):
            qbuf[base + n] = (rope(linear[n]) * scale).astype(jnp.bfloat16)

    tok_send = remote(tok_ref, tokbuf.at[1], misc_send.at[0], misc_sem.at[1], partner)
    list_send = remote(lists_ref, lvmem, misc_send.at[1], misc_sem.at[2], partner)

    def kv_wait(landed, number, side):
        number = 1 + 7 * side + number
        remote(landed, landed, kv_send.at[number], kv_recv.at[number], xp).wait_recv()

    def shared_wait(landed, number):
        remote(landed, landed, x_send.at[number], x_recv.at[number], xp).wait_recv()

    def run(op):
        kind, at = op[0], op[1:]
        if kind == "own":
            send_own(*at)
        elif kind == "z":
            pass_on(*at)
        elif kind == "yf":
            send_across(*at)
        elif kind == "y":
            wait_y(*at)
        elif kind == "kv0":
            if at[0] == 0:
                for copy in kv_loads:
                    copy.wait()
            else:
                other = kvbuf.at[ctx + 1 - 2 * core]
                remote(other, other, kv_send.at[0], kv_recv.at[0], partner).wait_recv()
            for number in range(3):
                kv_copy(number, at[0]).start()
        elif kind == "kv1":
            kv_wait(cached(x, 1 - y_hi, at[0]), 0, at[0])
            kv_copy(3, at[0]).start()
            kv_copy(4, at[0]).start()
        elif kind == "kv2":
            kv_wait(cached(left_x, y_hi, at[0]), 1, at[0])
            kv_copy(5, at[0]).start()
        elif kind == "kv3":
            kv_wait(cached(right_x, 1 - y_hi, at[0]), 4, at[0])
            kv_copy(6, at[0]).start()
        elif kind == "kvw":
            for side in range(2):
                kv_wait(cached(right_x, y_hi, side), 2, side)
                kv_wait(cached(left_x, 1 - y_hi, side), 3, side)
                kv_wait(cached(far_x, y_hi, side), 5, side)
                kv_wait(cached(far_x, 1 - y_hi, side), 6, side)
        elif kind == "b0":
            wait_y(0)
            for copy in x_copies[:4]:
                copy.start()
        elif kind == "b1":
            shared_wait(shared(left_x, 0), 0)
            shared_wait(shared(right_x, 1), 1)
            x_copies[4].start()
            x_copies[5].start()
        elif kind == "b2":
            shared_wait(shared(left_x, 1), 2)
            shared_wait(shared(right_x, 0), 3)
        elif kind == "b3":
            shared_wait(shared(far_x, 0), 4)
            shared_wait(shared(far_x, 1), 5)

    for copy in kv_parts:
        copy.start()
    for op in SCHEDULE[0][0][:AHEAD]:
        run(op)
    list_send.start()
    tok_send.start()
    table_load.wait()
    for copy in flat_loads:
        copy.wait()
    gain_ref[0:1, :] = flat_gain[...].astype(jnp.float32).reshape(1, gain_ref.shape[1])
    row = 0
    for flat in (flat_bq, flat_bk, flat_bv):
        for step in range(flat.shape[0] // HD):
            piece = flat[step * HD : (step + 1) * HD].astype(jnp.float32)
            bias_ref[row : row + 1, :] = piece.reshape(1, HD)
            row += 1

    pairs = (
        (10 + x, 4),
        (5, 6),
        (7, 8),
        (10 + left_x, 10 + right_x),
        (9, 10 + far_x),
    )
    units = [unit for _, unit in SCHEDULE]

    @pl.loop(0, len(SCHEDULE))
    def _(now):
        for number, (ops, _unused) in enumerate(SCHEDULE):
            rest = ops[AHEAD:] if number == 0 else ops
            if rest:

                @pl.when(now == number)
                def _():
                    for op in rest:
                        run(op)

        def on(kind):
            places = [n for n, unit in enumerate(units) if unit[0] == kind]
            condition = functools.reduce(jnp.logical_or, [now == n for n in places])

            def pick(values):
                value = values[units[places[-1]][1]]
                for n in places[:-1]:
                    value = jnp.where(now == n, values[units[n][1]], value)
                return value

            return condition, pick

        @pl.when(on("N0")[0])
        def _():
            tok_load.wait()
            norm_rows(0)

        @pl.when(on("T")[0])
        def _():
            tables()

        @pl.when(on("N1")[0])
        def _():
            tok_send.wait_recv()
            norm_rows(1)
            list_send.wait_recv()
            list_load.wait()
            move = pltpu.make_async_copy(lvmem, lsmem.at[1], misc_sem.at[4])
            move.start()
            move.wait()

        condition, pick_pair = on("K")

        @pl.when(condition)
        def _():
            key_value_chunks(pick_pair((0, 1)))

        condition, pick_query = on("P")

        @pl.when(condition)
        def _():
            query_chunks(
                pick_query([first for first, _ in pairs]),
                pick_query([second for _, second in pairs]),
                0,
            )

        @pl.when(on("X")[0])
        def _():
            query_chunks(*pairs[1], 2)
            attend(pairs[3], 0)

        condition, pick_heads = on("A")

        @pl.when(condition)
        def _():
            attend(
                (
                    pick_heads([first for first, _ in pairs]),
                    pick_heads([second for _, second in pairs]),
                ),
                pick_heads((0, 2, 0, 0, 0)),
            )

    for i in range(CHUNKS):
        sent = wbuf.at[0, 0:14] if i in Y_FIRST else wbuf.at[0, 0:7]
        pltpu.make_async_copy(sent, sent, z_send.at[i]).wait()
        sent = wbuf.at[0, 0] if i in Y_FIRST else wbuf.at[0, 0:8]
        pltpu.make_async_copy(sent, sent, y_send.at[i]).wait()

    for copy in x_copies:
        copy.wait_send()
    pltpu.make_async_copy(kvbuf.at[0], kvbuf.at[0], kv_send.at[0]).wait()
    for side in range(2):
        for number in range(7):
            kv_copy(number, side).wait_send()
    tok_send.wait_send()
    list_send.wait_send()
    written = ostage
    pltpu.make_async_copy(written, written, out_send.at[0]).wait()
    pltpu.make_async_copy(written, written, out_recv.at[0]).wait()


def write_kernel(source, ctx_ref, keys_ref, values_ref, sem):
    copies = []
    rows = source.shape[0] // 4
    for part in range(4):
        at = slice(part * rows, (part + 1) * rows)
        for n, (target, first) in enumerate(((ctx_ref, 0), (keys_ref, 20), (values_ref, 24))):
            column = slice(first * HD, first * HD + target.shape[1])
            copies.append(
                pltpu.make_async_copy(
                    source.at[at, column], target.at[at, :], sem.at[part * 3 + n]
                )
            )
    for copy in copies:
        copy.start()
    for copy in copies:
        copy.wait()


def on_device(
    tokens,
    norm_gain,
    w_query,
    w_key,
    w_value,
    b_query,
    b_key,
    b_value,
    cache_keys,
    cache_values,
    block_lists,
    start_position,
):
    rows, features = tokens.shape
    shard = w_query.shape[0]
    lists = jnp.transpose(block_lists, (1, 2, 0))
    table = jnp.asarray(np.pad(angle_tables(HD), ((0, 4), (0, 0))), jnp.float32)
    hbm = pl.BlockSpec(memory_space=pltpu.HBM)
    vmem = pl.BlockSpec(memory_space=pltpu.VMEM)
    smem = pl.BlockSpec(memory_space=pltpu.SMEM)
    dma = pltpu.SemaphoreType.DMA
    heads_out = pl.pallas_call(
        kernel,
        out_shape=pltpu.VMEM((rows, 28 * HD), jnp.float32),
        in_specs=[smem] + [hbm] * 12,
        out_specs=pl.BlockSpec(memory_space=pltpu.VMEM),
        scratch_shapes=[
            pltpu.VMEM((14, 16, shard, HD), jnp.bfloat16),
            pltpu.VMEM((16, 4, QBLK, HD), jnp.bfloat16),
            pltpu.VMEM((2, rows, features), jnp.bfloat16),
            pltpu.VMEM((2 * rows, features), jnp.bfloat16),
            pltpu.VMEM((2 * rows, HD), jnp.float32),
            pltpu.VMEM((2 * rows, HD), jnp.float32),
            pltpu.VMEM((4, 2 * rows, HD), jnp.bfloat16),
            pltpu.VMEM((2, 2 * rows, HD), jnp.bfloat16),
            pltpu.VMEM((2, 2 * rows, HD), jnp.bfloat16),
            pltpu.VMEM((14, rows, HD), jnp.float32),
            pltpu.VMEM((8, features), jnp.float32),
            pltpu.VMEM((32, HD), jnp.float32),
            pltpu.VMEM(norm_gain.shape, jnp.bfloat16),
            pltpu.VMEM(b_query.shape, jnp.bfloat16),
            pltpu.VMEM(b_key.shape, jnp.bfloat16),
            pltpu.VMEM(b_value.shape, jnp.bfloat16),
            pltpu.VMEM((8, HD), jnp.float32),
            pltpu.VMEM(lists.shape, jnp.int32),
            pltpu.SMEM((2,) + lists.shape, jnp.int32),
            dma((CHUNKS,)),
            dma((CHUNKS, 8)),
            dma((8,)),
            dma((CHUNKS,)),
            dma((CHUNKS,)),
            dma((CHUNKS,)),
            dma((6,)),
            dma((6,)),
            dma((4,)),
            dma((15,)),
            dma((15,)),
            dma((10,)),
            dma((2,)),
            dma((1,)),
            dma((1,)),
        ],
        compiler_params=pltpu.CompilerParams(
            collective_id=0, has_side_effects=True, vmem_limit_bytes=58 << 20
        ),
        name="gather_attend",
    )(
        start_position,
        tokens,
        w_query,
        w_key,
        w_value,
        cache_keys,
        cache_values,
        lists,
        norm_gain,
        b_query,
        b_key,
        b_value,
        table,
    )
    return pl.pallas_call(
        write_kernel,
        out_shape=(
            jax.ShapeDtypeStruct((rows, 20 * HD), jnp.float32),
            jax.ShapeDtypeStruct((rows, 4 * HD), jnp.float32),
            jax.ShapeDtypeStruct((rows, 4 * HD), jnp.float32),
        ),
        in_specs=[vmem],
        out_specs=[hbm] * 3,
        scratch_shapes=[dma((12,))],
        compiler_params=pltpu.CompilerParams(vmem_limit_bytes=4 << 20),
        name="write_out",
    )(heads_out)


def solution(mesh):
    in_specs = (
        P(("ctx", "grp"), None),
        P(),
        P("grp", None),
        P("grp", None),
        P("grp", None),
        P(),
        P(),
        P(),
        P("ctx", None),
        P("ctx", None),
        P(None, ("ctx", "grp"), None),
        P(),
    )
    out_specs = (P(("ctx", "grp"), None), P(("ctx", "grp"), None), P(("ctx", "grp"), None))
    return jax.shard_map(
        on_device, mesh=mesh, in_specs=in_specs, out_specs=out_specs, check_vma=False
    )
```
